768 devices in a mesh: len: 96 (over x, z, y_hi), xs: 8 (over y_lo, core).
Axes of the slice: x: 4, y: 8 (y_hi: 2, y_lo: 4; y = y_hi * 4 + y_lo), z: 12, core: 2. Of those that a mesh axis runs over, the one named last changes fastest.
Arguments:
- alpha: float32 [768, 256, 256], P('len', 'xs'), may hold values from 0 to 1
- velocity: float32 [3, 768, 256, 256], P(None, 'len', 'xs'), may hold values from -4 to 4
- upwind: int32 [3, 768, 256, 256], P(None, 'len', 'xs'), may hold values 0 or 1
- celltype: int32 [768, 256, 256], P('len', 'xs'), may hold values from 0 to 3
- owner: int32 [256, 256], P('xs'), may hold values from 0 to 15
- lam_alpha: float32 [768, 256, 256], P('len', 'xs'), may hold values from -6 to 6
- lam_press: float32 [768, 256, 256], P('len', 'xs'), may hold values from -6 to 6
Outputs:
- grad_alpha: float32 [768, 256, 256], P('len', 'xs')
- grad_velocity: float32 [3, 768, 256, 256], P(None, 'len', 'xs')
- adjoint_pressure: float32 [768, 256, 256], P('len', 'xs')
- inlet_sens: float32 [16], replicated
The draws below stay inside these ranges and needn't reach their ends.
Inputs may be any that keep to these rules, and one draw needn't show every extreme that they name: `celltype`: cell type codes. `owner`: port indices.
All inputs are finite; a program needn't handle non-finite values. No bound on the sum of `upwind` on one device may be relied on, other than what follows from the above.
Results may differ from the reference program's by a relative error of at most 0.00024.
Values sent between devices are 32-bit elements; how exact they have to be, the bound alone decides.
No kernel may reach another device: no remote copies, remote signals or barrier semaphores. Data moves between devices by JAX's collectives and lax.ppermute only.
A program may use at most 32 MiB of HBM per device.

```python
import math
import jax
import jax.numpy as jnp
from jax import lax

SWEEPS = 2
PORTS = 16
NL = 768
NY = 256
NZ = 256
TOTAL_CELLS = 50331648


def with_ends(array, own_key, smallest, largest):
    shape = array.shape
    place = [jax.random.randint(jax.random.fold_in(own_key, axis), (), 0, shape[axis]) for axis in range(len(shape))]
    array = array.at[tuple(place)].set(smallest)
    longest = shape.index(max(shape))
    place[longest] = (place[longest] + 1) % shape[longest]
    return array.at[tuple(place)].set(largest)


def shard_levels(own_key, shape, split, smallest, high):
    gain = 1.0
    for dim, shards_of in split:
        steps = jax.random.uniform(jax.random.fold_in(jax.random.fold_in(own_key, 6), dim), (shards_of,), jnp.float32, smallest / len(split), high / len(split))
        gain = gain * jnp.repeat(jnp.exp(steps), shape[dim] // shards_of).reshape((-1,) + (1,) * (len(shape) - 1 - dim))
    return gain


def centred(own_key, shape, scale, reach, split=(), held_as=jnp.bfloat16):
    drawn = jax.random.normal(own_key, shape, jnp.float32) * scale
    if len(split) > 0:
        drawn = shard_levels(own_key, shape, split, -0.22, 0.18) * drawn
    return jnp.clip(drawn, min=-reach, max=reach).astype(held_as)


def setup_inputs(seed: int = 0) -> dict:
    streams_of = jax.random.split(jax.random.key(seed), 8)
    alpha = jnp.clip(1.0 * jax.random.uniform(streams_of[0], (NL, NY, NZ), jnp.float32) ** shard_levels(streams_of[0], (NL, NY, NZ), ((0, 96), (1, 8)), -0.2, 0.2), 0.0, 1.0)
    velocity = centred(streams_of[1], (3, NL, NY, NZ), 1.0, 4.0, ((1, 96), (2, 8)), jnp.float32)
    upwind = with_ends((jax.random.randint(streams_of[2], (3, NL, NY, NZ), 0, 2) < 1).astype(jnp.int32), jax.random.fold_in(streams_of[2], 1), 0, 1)
    celltype = with_ends(jax.random.randint(streams_of[3], (NL, NY, NZ), 0, 4), jax.random.fold_in(streams_of[3], 1), 0, 3).astype(jnp.int32)
    owner = with_ends(jax.random.randint(streams_of[4], (NY, NZ), 0, PORTS), jax.random.fold_in(streams_of[4], 1), 0, PORTS - 1).astype(jnp.int32)
    lam_alpha = centred(streams_of[5], (NL, NY, NZ), 1.0, 6.0, ((0, 96), (1, 8)), jnp.float32)
    lam_press = centred(streams_of[6], (NL, NY, NZ), 1.0, 6.0, ((0, 96), (1, 8)), jnp.float32)
    return {"alpha": alpha, "velocity": velocity, "upwind": upwind, "celltype": celltype, "owner": owner, "lam_alpha": lam_alpha, "lam_press": lam_press}


def upper(field, axis):
    pads = [(0, 0)] * field.ndim
    pads[axis] = (0, 1)
    padded = jnp.pad(field, pads)
    return jax.lax.slice_in_dim(padded, 1, field.shape[axis] + 1, axis=axis)

def lower(field, axis):
    pads = [(0, 0)] * field.ndim
    pads[axis] = (1, 0)
    padded = jnp.pad(field, pads)
    return jax.lax.slice_in_dim(padded, 0, field.shape[axis], axis=axis)

def reference(alpha, velocity, upwind, celltype, owner, lam_alpha, lam_press):
    opened = (celltype != 1).astype(jnp.float32)
    active = ((celltype == 0) | (celltype == 2)).astype(jnp.float32)
    inlet = (celltype == 2).astype(jnp.float32)
    rho = 1.0 + 9.0 * alpha
    total = lam_alpha
    grads = []
    k_high = []
    k_low = []
    for axis in range(3):
        flow = upwind[axis].astype(jnp.float32)
        alpha_next = upper(alpha, axis)
        open_next = upper(opened, axis)
        face = 0.4 * velocity[axis] * (upper(lam_alpha, axis) - lam_alpha) * (opened * open_next)
        grads.append(face * (flow * alpha + (1.0 - flow) * alpha_next))
        total = total + face * flow + lower(face * (1.0 - flow), axis)
        coeff = 2.0 * (opened * open_next) / (rho + (1.0 + 9.0 * alpha_next))
        k_high.append(coeff)
        k_low.append(lower(coeff, axis))
    grad_alpha = opened * total
    diag = 0.5 + (k_high[0] + k_high[1] + k_high[2]) + (k_low[0] + k_low[1] + k_low[2])
    rhs = lam_press + grad_alpha
    press = active * rhs / diag
    for sweep in range(SWEEPS):
        beside = k_high[0] * upper(press, 0) + k_low[0] * lower(press, 0)
        beside = beside + k_high[1] * upper(press, 1) + k_low[1] * lower(press, 1)
        beside = beside + k_high[2] * upper(press, 2) + k_low[2] * lower(press, 2)
        press = active * (rhs + beside) / diag
    column = lax.optimization_barrier(jnp.sum((lam_alpha + press) * inlet, axis=0))
    sens = jax.ops.segment_sum(column.reshape(-1), owner.reshape(-1).astype(jnp.int32), num_segments=PORTS)
    sens = sens / math.sqrt(TOTAL_CELLS)
    return (grad_alpha, jnp.stack(grads), press, sens)
```

```python
import math

import jax
import jax.numpy as jnp
from jax import lax
from jax.sharding import Mesh
from jax.sharding import PartitionSpec as P

SWEEPS = 2
PORTS = 16
LEN = ("x", "z", "yh")
XS = ("yl", "c")
SIZES = {"x": 4, "z": 12, "yh": 2, "yl": 4, "c": 2}


def size_of(axes):
    return math.prod(SIZES[a] for a in axes)


def shift(x, axes, by):
    count = size_of(axes)
    pairs = [(i, i + by) for i in range(count) if 0 <= i + by < count]
    return lax.ppermute(x, axes, pairs)


def cut(x, axis, index):
    return lax.slice_in_dim(x, index, index + 1, axis=axis)


def neighbours(x, axis, before, after):
    length = x.shape[axis]
    down = jnp.concatenate([before, lax.slice_in_dim(x, 0, length - 1, axis=axis)], axis=axis)
    up = jnp.concatenate([lax.slice_in_dim(x, 1, length, axis=axis), after], axis=axis)
    return down, up


def edges(x):
    last = [x.shape[0] - 1, x.shape[1] - 1]
    len_before = shift(cut(x, 0, last[0]), LEN, 1)
    len_after = shift(cut(x, 0, 0), LEN, -1)
    xs_before = shift(cut(x, 1, last[1]), XS, 1)
    xs_after = shift(cut(x, 1, 0), XS, -1)
    zero = jnp.zeros_like(cut(x, 2, 0))
    return [(len_before, len_after), (xs_before, xs_after), (zero, zero)]


def total_over(x, axes):
    count = size_of(axes)
    copies = jnp.broadcast_to(x[None], (count,) + x.shape)
    return jnp.sum(lax.all_to_all(copies, axes, 0, 0, tiled=True), axis=0)


def body(alpha, velocity, upwind, celltype, owner, lam_alpha, lam_press):
    opened = (celltype != 1).astype(jnp.float32)
    active = ((celltype == 0) | (celltype == 2)).astype(jnp.float32)
    inlet = (celltype == 2).astype(jnp.float32)
    flows = upwind.astype(jnp.float32)
    rho = 1.0 + 9.0 * alpha
    last = [alpha.shape[0] - 1, alpha.shape[1] - 1]
    passing = 0.4 * velocity * (1.0 - flows)

    def up_message(axis, axes):
        parts = [cut(v, axis, last[axis]) for v in (alpha, lam_alpha, opened, passing[axis])]
        return shift(jnp.concatenate(parts, axis=axis), axes, 1)

    def down_message(axis, axes):
        parts = [cut(v, axis, 0) for v in (alpha, lam_alpha, opened)]
        return shift(jnp.concatenate(parts, axis=axis), axes, -1)

    befores = [up_message(0, LEN), up_message(1, XS), None]
    afters = [down_message(0, LEN), down_message(1, XS), None]
    zero = jnp.zeros_like(cut(alpha, 2, 0))
    befores[2] = jnp.concatenate([zero] * 4, axis=2)
    afters[2] = jnp.concatenate([zero] * 3, axis=2)
    total = lam_alpha
    grads = []
    k_high = []
    k_low = []
    for axis in range(3):
        flow = flows[axis]
        a_b, l_b, o_b, p_b = (cut(befores[axis], axis, i) for i in range(4))
        a_a, l_a, o_a = (cut(afters[axis], axis, i) for i in range(3))
        alpha_prev, alpha_next = neighbours(alpha, axis, a_b, a_a)
        _, lam_next = neighbours(lam_alpha, axis, l_b, l_a)
        open_prev, open_next = neighbours(opened, axis, o_b, o_a)
        face = 0.4 * velocity[axis] * (lam_next - lam_alpha) * (opened * open_next)
        grads.append(face * (flow * alpha + (1.0 - flow) * alpha_next))
        passed = face * (1.0 - flow)
        edge = p_b * (cut(lam_alpha, axis, 0) - l_b) * (o_b * cut(opened, axis, 0))
        incoming, _ = neighbours(passed, axis, edge, zero if axis == 2 else edge)
        total = total + face * flow + incoming
        k_high.append(2.0 * (opened * open_next) / (rho + (1.0 + 9.0 * alpha_next)))
        k_low.append(2.0 * (open_prev * opened) / (1.0 + 9.0 * alpha_prev + rho))
    grad_alpha = opened * total
    grad_velocity = jnp.stack(grads)
    diag = 0.5 + (k_high[0] + k_high[1] + k_high[2]) + (k_low[0] + k_low[1] + k_low[2])
    rhs = lam_press + grad_alpha
    press = active * rhs / diag
    for _ in range(SWEEPS):
        sides = edges(press)
        beside = 0.0
        for axis in range(3):
            down, up = neighbours(press, axis, *sides[axis])
            beside = beside + k_high[axis] * up + k_low[axis] * down
        press = active * (rhs + beside) / diag
    column = jnp.sum((lam_alpha + press) * inlet, axis=0)
    ports = jnp.arange(PORTS, dtype=jnp.int32)
    sens = jnp.sum(jnp.where(owner[None] == ports[:, None, None], column[None], 0.0), axis=(1, 2))
    sens = total_over(sens, ("x", "z"))
    sens = total_over(sens, ("yh", "yl", "c"))
    cells = math.prod(alpha.shape) * size_of(LEN + XS)
    return (grad_alpha, grad_velocity, press, sens / math.sqrt(cells))


def solution(mesh):
    parts = Mesh(mesh.devices.reshape(tuple(SIZES.values())), tuple(SIZES))
    field = P(LEN, XS, None)
    faces = P(None, LEN, XS, None)
    in_specs = (field, faces, faces, field, P(XS, None), field, field)
    out_specs = (field, faces, field, P())
    return jax.shard_map(body, mesh=parts, in_specs=in_specs, out_specs=out_specs, check_vma=False)
```

```python
import functools
import math

import jax
import jax.numpy as jnp
from jax import lax
from jax.experimental import pallas as pl
from jax.experimental.pallas import tpu as pltpu
from jax.sharding import Mesh
from jax.sharding import PartitionSpec as P

SWEEPS = 2
PORTS = 16
LEN = ("x", "z", "yh")
XS = ("yl", "c")
FIRST = ("x", "yh", "yl")
SECOND = ("z", "c")
SIZES = {"x": 4, "z": 12, "yh": 2, "yl": 4, "c": 2}
PLANES = 8
ROWS = 32
HALO = 8
EXT = ROWS + HALO
NZ = 256
WALL = 1e30
STRIP = (("t", 3), ("al", 3), ("la", 3), ("lp", 2), ("c0", 2), ("m0", 2), ("c1", 3), ("m1", 2), ("c2", 2), ("m2", 2))
FIELDS = [name for name, _ in STRIP]
DOWN_ROWS = 6 * ROWS + 2 * HALO
UP_ROWS = 8 * ROWS + 3 * HALO


def size_of(axes):
    return math.prod(SIZES[a] for a in axes)


def shift(x, axes, by):
    count = size_of(axes)
    pairs = [(i, i + by) for i in range(count) if 0 <= i + by < count]
    return lax.ppermute(x, axes, pairs)


def up_y(x):
    return pltpu.roll(x, EXT - 1, 0)


def down_y(x):
    return pltpu.roll(x, 1, 0)


def up_z(x):
    return pltpu.roll(x, NZ - 1, 1)


def down_z(x):
    return pltpu.roll(x, 1, 1)


def resistance(t, alpha):
    return jnp.where(t != 0.0, 1.0 + 9.0 * alpha, WALL)


def coupling(low, high):
    both = low + high
    through = both < 0.5 * WALL
    return through, jnp.where(through, 2.0 / both, 0.0)


def is_active(t):
    return jnp.abs(t) == 1.0


def split_flux(through, speed, donor, low, high):
    face = jnp.where(through, speed * (high - low), 0.0)
    stays = face * donor
    return stays, face - stays


def lanes(shape):
    return lax.broadcasted_iota(jnp.int32, shape, 1)


def sublanes(shape):
    return lax.broadcasted_iota(jnp.int32, shape, 0)


def strip_kernel(al_l, ve_l, up_l, ct_l, la_l, lp_l, al_f, ve_f, up_f, ct_f, la_f, lp_f, to_next, to_prev):
    for out, al, ve, up, ct, la, lp, last in (
        (to_next, al_l, ve_l, up_l, ct_l, la_l, lp_l, True),
        (to_prev, al_f, ve_f, up_f, ct_f, la_f, lp_f, False),
    ):
        at = 0
        for name, count in STRIP:
            first = HALO - count if last else 0
            rows = pl.ds(first, count)
            if name == "t":
                value = ct[:, rows, :].astype(jnp.float32) - 1.0
            elif name == "al":
                value = al[:, rows, :]
            elif name == "la":
                value = la[:, rows, :]
            elif name == "lp":
                value = lp[:, rows, :]
            elif name[0] == "c":
                value = 0.4 * ve[int(name[1]), :, rows, :]
                if name == "c1" and last:
                    donor = up[1, :, rows, :].astype(jnp.float32)
                    row = lax.broadcasted_iota(jnp.int32, value.shape, 1)
                    value = jnp.where(row == 0, value * (1.0 - donor), value)
            else:
                value = up[int(name[1]), :, rows, :].astype(jnp.float32)
            out[:, pl.ds(at, count), :] = value
            at += count


def strips(alpha, velocity, upwind, celltype, lam, lam_press):
    def block(x, last):
        index = x.shape[-2] // HALO - 1 if last else 0
        if x.ndim == 3:
            return pl.BlockSpec((PLANES, HALO, NZ), lambda i: (0, index, 0))
        return pl.BlockSpec((3, PLANES, HALO, NZ), lambda i: (0, 0, index, 0))

    args = (alpha, velocity, upwind, celltype, lam, lam_press)
    message = jax.ShapeDtypeStruct((PLANES, 24, NZ), jnp.float32)
    whole = pl.BlockSpec((PLANES, 24, NZ), lambda i: (0, 0, 0))
    return pl.pallas_call(
        strip_kernel,
        grid=(1,),
        in_specs=[block(x, True) for x in args] + [block(x, False) for x in args],
        out_specs=[whole, whole],
        out_shape=[message, message],
        name="strips",
    )(*args, *args)


class Own:
    def __init__(self, al, ve, up, ct, la, lp, halo):
        self.refs = (al, ve, up, ct, la, lp, halo)

    def get(self, name, p):
        al, ve, up, ct, la, lp, halo = self.refs
        if name == "t":
            own = ct[p].astype(jnp.float32) - 1.0
        elif name in ("al", "la", "lp"):
            own = {"al": al, "la": la, "lp": lp}[name][p]
        elif name[0] == "c":
            own = 0.4 * ve[int(name[1]), p]
        else:
            own = up[int(name[1]), p].astype(jnp.float32)
        return jnp.concatenate([own, halo[FIELDS.index(name), p]], axis=0)

    def resist(self, p):
        return resistance(self.get("t", p), self.get("al", p))


def in_plane(r):
    through_y, ky = coupling(r, up_y(r))
    through_z, kz = coupling(r, up_z(r))
    inside = lanes(r.shape) < NZ - 1
    return through_y, ky, through_z & inside, jnp.where(inside, kz, 0.0)


def in_plane_terms(own, p, r):
    through_y, ky, through_z, kz = in_plane(r)
    la = own.get("la", p)
    stays, passes = split_flux(through_y, own.get("c1", p), own.get("m1", p), la, up_y(la))
    flux = stays + down_y(passes)
    stays, passes = split_flux(through_z, own.get("c2", p), own.get("m2", p), la, up_z(la))
    flux = flux + (stays + down_z(passes))
    return flux, ky + down_y(ky), kz + down_z(kz), ky, kz


def between(own, p):
    through, k = coupling(own.resist(p), own.resist(p + 1))
    stays, passes = split_flux(through, own.get("c0", p), own.get("m0", p), own.get("la", p), own.get("la", p + 1))
    return k, stays, passes


def fill_halo(prev, nxt, halo):
    at = 0
    halo[...] = jnp.zeros(halo.shape, jnp.float32)
    for f, (_, count) in enumerate(STRIP):
        halo[f, :, pl.ds(0, count), :] = nxt[:, pl.ds(at, count), :]
        halo[f, :, pl.ds(HALO - count, count), :] = prev[:, pl.ds(at, count), :]
        at += count


def pack_pair(a, b):
    row = sublanes(a.shape)
    low = (row == 2) | (row == 3)
    high = (row == 4) | (row == 5)
    return jnp.where(low, pltpu.roll(b, 2, 0), jnp.where(high, pltpu.roll(b, HALO - 2, 0), a))


def pack_trio(a, b, c):
    row = sublanes(a.shape)
    out = jnp.where(row == 2, pltpu.roll(b, 2, 0), a)
    out = jnp.where(row == 5, pltpu.roll(b, HALO - 2, 0), out)
    out = jnp.where(row == 3, pltpu.roll(c, 3, 0), out)
    return jnp.where(row == 4, pltpu.roll(c, HALO - 3, 0), out)


def outer(a):
    row = sublanes(a.shape)
    return jnp.where((row < 2) | (row > 5), a, 0.0)


def unpack_pair(tile):
    row = sublanes(tile.shape)
    b = jnp.where(row < 2, pltpu.roll(tile, HALO - 2, 0), jnp.where(row > 5, pltpu.roll(tile, 2, 0), 0.0))
    return outer(tile), b


def unpack_trio(tile):
    row = sublanes(tile.shape)
    b = jnp.where(row == 0, pltpu.roll(tile, HALO - 2, 0), jnp.where(row == 7, pltpu.roll(tile, 2, 0), 0.0))
    c = jnp.where(row == 0, pltpu.roll(tile, HALO - 3, 0), jnp.where(row == 7, pltpu.roll(tile, 3, 0), 0.0))
    return outer(tile), b, c


def slab_kernel(al, ve, up, ct, la, lp, prev, nxt, halo, down, upper):
    fill_halo(prev, nxt, halo)
    own = Own(al, ve, up, ct, la, lp, halo)
    top = PLANES - 1
    for out, edge, inner, far in ((down, 0, 1, 2), (upper, top, top - 1, top - 2)):
        low, lower_far = (edge, inner) if edge == 0 else (inner, far)
        k_edge, stays_edge, passes_edge = between(own, low)
        k_far, stays_far, passes_far = between(own, lower_far)
        if edge == 0:
            edge_flux, inner_flux = stays_edge, passes_edge + stays_far
        else:
            edge_flux, inner_flux = passes_edge, stays_edge + passes_far

        def sums(p, flux_len, k_len):
            flux, sum_y, sum_z, _, _ = in_plane_terms(own, p, own.resist(p))
            t = own.get("t", p)
            source = own.get("lp", p) + jnp.where(t != 0.0, own.get("la", p) + (flux_len + flux), 0.0)
            return t, source, 0.5 + (k_len + sum_y + sum_z)

        t_in, source_in, diag_in = sums(inner, inner_flux, k_edge + k_far)
        carried = k_edge * jnp.where(is_active(t_in), source_in / diag_in, 0.0)
        t, source, diag = sums(edge, edge_flux, k_edge)
        alpha, lam = own.get("al", edge), own.get("la", edge)
        planes = [t, alpha, lam, source, diag, carried]
        tiles = [pack_pair(t[ROWS:], alpha[ROWS:]), pack_trio(lam[ROWS:], source[ROWS:], diag[ROWS:])]
        if edge != 0:
            speed, donor = own.get("c0", edge), own.get("m0", edge)
            planes += [speed, donor]
            tiles.append(pack_pair(speed[ROWS:], donor[ROWS:]))
        for i, plane in enumerate(planes):
            out[pl.ds(i * ROWS, ROWS), :] = plane[:ROWS]
        for i, tile in enumerate(tiles):
            out[pl.ds(len(planes) * ROWS + i * HALO, HALO), :] = tile


def slabs(alpha, velocity, upwind, celltype, lam, lam_press, prev, nxt):
    return pl.pallas_call(
        slab_kernel,
        out_shape=[
            jax.ShapeDtypeStruct((len(FIELDS), PLANES, HALO, NZ), jnp.float32),
            jax.ShapeDtypeStruct((DOWN_ROWS, NZ), jnp.float32),
            jax.ShapeDtypeStruct((UP_ROWS, NZ), jnp.float32),
        ],
        name="slabs",
    )(alpha, velocity, upwind, celltype, lam, lam_press, prev, nxt)


def read_message(ref, with_faces):
    count = 8 if with_faces else 6
    planes = [ref[pl.ds(i * ROWS, ROWS), :] for i in range(count)]
    tiles = [ref[pl.ds(count * ROWS + i * HALO, HALO), :] for i in range(count // 2 - 1)]
    t, alpha = unpack_pair(tiles[0])
    lam, source, diag = unpack_trio(tiles[1])
    halos = [t, alpha, lam, source, diag, jnp.zeros_like(t)]
    if with_faces:
        halos += list(unpack_pair(tiles[2]))
    return [jnp.concatenate([a, b], axis=0) for a, b in zip(planes, halos)]


def relax_kernel(
    al, ve, up, ct, la, lp, ow, halo, below, above, grad, press, sums, kl, ky, kz, source, scale, first, second
):
    own = Own(al, ve, up, ct, la, lp, halo)
    t_b, al_b, la_b, src_b, diag_b, carried_b, c_b, m_b = read_message(below, True)
    t_a, al_a, la_a, src_a, diag_a, carried_a = read_message(above, False)
    r_b, r_a = resistance(t_b, al_b), resistance(t_a, al_a)
    top = PLANES - 1

    def weight(t, diag):
        return jnp.where(is_active(t) & (diag >= 0.5), 1.0 / diag, 0.0)

    through, k = coupling(r_b, own.resist(0))
    stays, passes = split_flux(through, c_b, m_b, la_b, own.get("la", 0))
    kl[0] = k
    _, ky[0], _, kz[0] = in_plane(r_b)
    source[0] = src_b + stays
    scale[0] = weight(t_b, diag_b + k)
    first[0] = source[0] * scale[0]
    source[0] = source[0] + carried_b
    incoming = passes
    for p in range(PLANES):
        r = own.resist(p)
        lam = own.get("la", p)
        r_next = own.resist(p + 1) if p < top else r_a
        lam_next = own.get("la", p + 1) if p < top else la_a
        through, k = coupling(r, r_next)
        stays, passes = split_flux(through, own.get("c0", p), own.get("m0", p), lam, lam_next)
        flux, sum_y, sum_z, k_y, k_z = in_plane_terms(own, p, r)
        t = own.get("t", p)
        total = jnp.where(t != 0.0, lam + ((incoming + stays) + flux), 0.0)
        grad[p] = total[:ROWS]
        kl[p + 1], ky[p + 1], kz[p + 1] = k, k_y, k_z
        source[p + 1] = own.get("lp", p) + total
        scale[p + 1] = weight(t, 0.5 + ((k + kl[p]) + sum_y + sum_z))
        first[p + 1] = source[p + 1] * scale[p + 1]
        incoming = passes
    k = kl[PLANES]
    _, ky[PLANES + 1], _, kz[PLANES + 1] = in_plane(r_a)
    source[PLANES + 1] = src_a + incoming
    scale[PLANES + 1] = weight(t_a, diag_a + k)
    first[PLANES + 1] = source[PLANES + 1] * scale[PLANES + 1]
    source[PLANES + 1] = source[PLANES + 1] + carried_a

    def sweep(x, i):
        mid = x[i]
        k_y, k_z = ky[i], kz[i]
        beside = k_y * up_y(mid) + down_y(k_y) * down_y(mid)
        beside = beside + (k_z * up_z(mid) + down_z(k_z) * down_z(mid))
        if i <= PLANES:
            beside = beside + kl[i] * x[i + 1]
        if i > 0:
            beside = beside + kl[i - 1] * x[i - 1]
        return (source[i] + beside) * scale[i]

    for i in range(PLANES + 2):
        second[i] = sweep(first, i)
    column = jnp.zeros((ROWS, NZ), jnp.float32)
    for p in range(PLANES):
        x = sweep(second, p + 1)[:ROWS]
        press[p] = x
        column = column + jnp.where(ct[p] == 2, la[p] + x, 0.0)
    owner = ow[...]
    parts = []
    for port in range(PORTS):
        mine = jnp.where(owner == port, column, 0.0)
        mine = mine[:, :128] + mine[:, 128:]
        parts.append(jnp.sum(mine, axis=0, keepdims=True))
    table = jnp.sum(jnp.concatenate(parts, axis=0), axis=1, keepdims=True)
    diagonal = lanes((PORTS, 128)) == sublanes((PORTS, 128))
    line = jnp.sum(jnp.where(diagonal, table, 0.0), axis=0, keepdims=True)
    sums[...] = jnp.broadcast_to(line, sums.shape)


def relax(alpha, velocity, upwind, celltype, lam, lam_press, owner, halo, below, above):
    plane = functools.partial(pltpu.VMEM, dtype=jnp.float32)
    field = jax.ShapeDtypeStruct((PLANES, ROWS, NZ), jnp.float32)
    return pl.pallas_call(
        relax_kernel,
        out_shape=[field, field, jax.ShapeDtypeStruct((size_of(FIRST), 128), jnp.float32)],
        scratch_shapes=[plane((PLANES + 2, EXT, NZ)) for _ in range(7)],
        name="relax",
    )(alpha, velocity, upwind, celltype, lam, lam_press, owner, halo, below, above)


def faces_kernel(al, ve, up, ct, la, lp, halo, above, out):
    own = Own(al, ve, up, ct, la, lp, halo)
    t_a, al_a, la_a = read_message(above, False)[:3]
    r_a = resistance(t_a, al_a)

    def write(axis, p, through, speed, donor, lam, lam_next, alpha, alpha_next):
        face = jnp.where(through, speed * (lam_next - lam), 0.0)
        out[axis, p] = (face * jnp.where(donor != 0.0, alpha, alpha_next))[:ROWS]

    for p in range(PLANES):
        r, alpha, lam = own.resist(p), own.get("al", p), own.get("la", p)
        inner = p < PLANES - 1
        r_next = own.resist(p + 1) if inner else r_a
        alpha_next = own.get("al", p + 1) if inner else al_a
        lam_next = own.get("la", p + 1) if inner else la_a
        through, _ = coupling(r, r_next)
        write(0, p, through, own.get("c0", p), own.get("m0", p), lam, lam_next, alpha, alpha_next)
        through, _ = coupling(r, up_y(r))
        write(1, p, through, own.get("c1", p), own.get("m1", p), lam, up_y(lam), alpha, up_y(alpha))
        through, _ = coupling(r, up_z(r))
        through = through & (lanes(r.shape) < NZ - 1)
        write(2, p, through, own.get("c2", p), own.get("m2", p), lam, up_z(lam), alpha, up_z(alpha))


def faces(alpha, velocity, upwind, celltype, lam, lam_press, halo, above):
    return pl.pallas_call(
        faces_kernel,
        out_shape=jax.ShapeDtypeStruct((3, PLANES, ROWS, NZ), jnp.float32),
        name="faces",
    )(alpha, velocity, upwind, celltype, lam, lam_press, halo, above)


def total_over(copies, axes):
    return jnp.sum(lax.all_to_all(copies, axes, 0, 0, tiled=True), axis=0)


def body(alpha, velocity, upwind, celltype, owner, lam_alpha, lam_press):
    args = (alpha, velocity, upwind, celltype, lam_alpha, lam_press)
    to_next, to_prev = strips(*args)
    prev = shift(to_next, XS, 1)
    nxt = shift(to_prev, XS, -1)
    halo, down, upper = slabs(*args, prev, nxt)
    below = shift(upper, LEN, 1)
    above = shift(down, LEN, -1)
    grad_alpha, press, sums = relax(*args, owner, halo, below, above)
    grad_velocity = faces(*args, halo, above)
    sums = total_over(sums, FIRST)
    sums = total_over(jnp.broadcast_to(sums[None], (size_of(SECOND), 128)), SECOND)
    cells = math.prod(alpha.shape) * size_of(LEN + XS)
    return (grad_alpha, grad_velocity, press, sums[:PORTS] / math.sqrt(cells))


def solution(mesh):
    parts = Mesh(mesh.devices.reshape(tuple(SIZES.values())), tuple(SIZES))
    field = P(LEN, XS, None)
    faces_spec = P(None, LEN, XS, None)
    in_specs = (field, faces_spec, faces_spec, field, P(XS, None), field, field)
    out_specs = (field, faces_spec, field, P())
    return jax.shard_map(body, mesh=parts, in_specs=in_specs, out_specs=out_specs, check_vma=False)
```

```python
import functools
import math

import jax
import jax.numpy as jnp
from jax import lax
from jax.experimental import pallas as pl
from jax.experimental.pallas import tpu as pltpu
from jax.sharding import Mesh
from jax.sharding import PartitionSpec as P

SWEEPS = 2
PORTS = 16
LEN = ("x", "z", "yh")
XS = ("yl", "c")
FIRST = ("x", "yh", "yl")
SECOND = ("z", "c")
SIZES = {"x": 4, "z": 12, "yh": 2, "yl": 4, "c": 2}
PLANES = 8
ROWS = 32
HALO = 8
EXT = ROWS + HALO
NZ = 256
WALL = 1e30
VMEM_LIMIT = 16 * 2**20
SLAB_FLOPS = 20_000_000
SLAB_BYTES = 40_000_000
STRIP = (("t", 3), ("al", 3), ("la", 3), ("lp", 2), ("c0", 2), ("m0", 2), ("c1", 3), ("m1", 2), ("c2", 2), ("m2", 2))
FIELDS = [name for name, _ in STRIP]
EARLY_ROWS = 7 * ROWS
DOWN_ROWS = 5 * ROWS + 2 * HALO
UP_ROWS = 4 * HALO
PARAMS = pltpu.CompilerParams(vmem_limit_bytes=VMEM_LIMIT)


def size_of(axes):
    return math.prod(SIZES[a] for a in axes)


def shift(x, axes, by):
    count = size_of(axes)
    pairs = [(i, i + by) for i in range(count) if 0 <= i + by < count]
    return lax.ppermute(x, axes, pairs)


def up_y(x):
    return pltpu.roll(x, EXT - 1, 0)


def down_y(x):
    return pltpu.roll(x, 1, 0)


def up_z(x):
    return pltpu.roll(x, NZ - 1, 1)


def down_z(x):
    return pltpu.roll(x, 1, 1)


def resistance(t, alpha):
    return jnp.where(t != 0.0, 1.0 + 9.0 * alpha, WALL)


def coupling(low, high):
    both = low + high
    through = both < 0.5 * WALL
    return through, jnp.where(through, 2.0 / both, 0.0)


def is_active(t):
    return jnp.abs(t) == 1.0


def split_flux(through, speed, donor, low, high):
    face = jnp.where(through, speed * (high - low), 0.0)
    stays = face * donor
    return stays, face - stays


def lanes(shape):
    return lax.broadcasted_iota(jnp.int32, shape, 1)


def sublanes(shape):
    return lax.broadcasted_iota(jnp.int32, shape, 0)


def strip_kernel(al, ve, up, ct, la, lp, to_next, to_prev, *scratch):
    sem = scratch[-1]
    last, first = scratch[:6], scratch[6:12]
    copies = []
    for kept, start in ((last, ROWS - HALO), (first, 0)):
        for source, target in zip((al, ve, up, ct, la, lp), kept):
            rows = pl.ds(start, HALO)
            window = source.at[:, rows, :] if len(source.shape) == 3 else source.at[:, :, rows, :]
            copies.append(pltpu.make_async_copy(window, target, sem.at[len(copies)]))
            copies[-1].start()
    for copy in copies:
        copy.wait()
    for out, kept, is_last in ((to_next, last, True), (to_prev, first, False)):
        al_k, ve_k, up_k, ct_k, la_k, lp_k = kept
        at = 0
        for name, count in STRIP:
            rows = pl.ds(HALO - count if is_last else 0, count)
            if name == "t":
                value = ct_k[:, rows, :].astype(jnp.float32) - 1.0
            elif name in ("al", "la", "lp"):
                value = {"al": al_k, "la": la_k, "lp": lp_k}[name][:, rows, :]
            elif name[0] == "c":
                value = 0.4 * ve_k[int(name[1]), :, rows, :]
                if name == "c1" and is_last:
                    donor = up_k[1, :, rows, :].astype(jnp.float32)
                    row = lax.broadcasted_iota(jnp.int32, value.shape, 1)
                    value = jnp.where(row == 0, value * (1.0 - donor), value)
            else:
                value = up_k[int(name[1]), :, rows, :].astype(jnp.float32)
            out[:, pl.ds(at, count), :] = value
            at += count


def strips(*args):
    message = jax.ShapeDtypeStruct((PLANES, 24, NZ), jnp.float32)
    kept = [pltpu.VMEM(x.shape[:-2] + (HALO, NZ), x.dtype) for x in args]
    return pl.pallas_call(
        strip_kernel,
        in_specs=[pl.BlockSpec(memory_space=pltpu.HBM)] * 6,
        out_shape=[message, message],
        scratch_shapes=kept + kept + [pltpu.SemaphoreType.DMA((12,))],
        compiler_params=PARAMS,
        name="strips",
    )(*(pltpu.with_memory_space_constraint(x, pltpu.HBM) for x in args))


class Own:
    def __init__(self, al, ve, up, ct, la, lp, halo):
        self.refs = (al, ve, up, ct, la, lp, halo)

    def get(self, name, p):
        al, ve, up, ct, la, lp, halo = self.refs
        if name == "t":
            own = ct[p].astype(jnp.float32) - 1.0
        elif name in ("al", "la", "lp"):
            own = {"al": al, "la": la, "lp": lp}[name][p]
        elif name[0] == "c":
            own = 0.4 * ve[int(name[1]), p]
        else:
            own = up[int(name[1]), p].astype(jnp.float32)
        tile = jnp.zeros((HALO, NZ), jnp.float32) if halo is None else halo[FIELDS.index(name), p]
        return jnp.concatenate([own, tile], axis=0)

    def resist(self, p):
        return resistance(self.get("t", p), self.get("al", p))


def in_plane(r):
    through_y, ky = coupling(r, up_y(r))
    through_z, kz = coupling(r, up_z(r))
    inside = lanes(r.shape) < NZ - 1
    return through_y, ky, through_z & inside, jnp.where(inside, kz, 0.0)


def in_plane_terms(own, p, r):
    through_y, ky, through_z, kz = in_plane(r)
    la = own.get("la", p)
    stays, passes = split_flux(through_y, own.get("c1", p), own.get("m1", p), la, up_y(la))
    flux = stays + down_y(passes)
    stays, passes = split_flux(through_z, own.get("c2", p), own.get("m2", p), la, up_z(la))
    flux = flux + (stays + down_z(passes))
    return flux, ky + down_y(ky), kz + down_z(kz), ky, kz


def between(own, p):
    through, k = coupling(own.resist(p), own.resist(p + 1))
    stays, passes = split_flux(through, own.get("c0", p), own.get("m0", p), own.get("la", p), own.get("la", p + 1))
    return k, stays, passes


def fill_halo(prev, nxt, halo):
    at = 0
    halo[...] = jnp.zeros(halo.shape, jnp.float32)
    for f, (_, count) in enumerate(STRIP):
        halo[f, :, pl.ds(0, count), :] = nxt[:, pl.ds(at, count), :]
        halo[f, :, pl.ds(HALO - count, count), :] = prev[:, pl.ds(at, count), :]
        at += count


def pack_pair(a, b):
    row = sublanes(a.shape)
    low = (row == 2) | (row == 3)
    high = (row == 4) | (row == 5)
    return jnp.where(low, pltpu.roll(b, 2, 0), jnp.where(high, pltpu.roll(b, HALO - 2, 0), a))


def pack_trio(a, b, c):
    row = sublanes(a.shape)
    out = jnp.where(row == 2, pltpu.roll(b, 2, 0), a)
    out = jnp.where(row == 5, pltpu.roll(b, HALO - 2, 0), out)
    out = jnp.where(row == 3, pltpu.roll(c, 3, 0), out)
    return jnp.where(row == 4, pltpu.roll(c, HALO - 3, 0), out)


def outer(a):
    row = sublanes(a.shape)
    return jnp.where((row < 2) | (row > 5), a, 0.0)


def unpack_pair(tile):
    row = sublanes(tile.shape)
    b = jnp.where(row < 2, pltpu.roll(tile, HALO - 2, 0), jnp.where(row > 5, pltpu.roll(tile, 2, 0), 0.0))
    return outer(tile), b


def unpack_trio(tile):
    row = sublanes(tile.shape)
    b = jnp.where(row == 0, pltpu.roll(tile, HALO - 2, 0), jnp.where(row == 7, pltpu.roll(tile, 2, 0), 0.0))
    c = jnp.where(row == 0, pltpu.roll(tile, HALO - 3, 0), jnp.where(row == 7, pltpu.roll(tile, 3, 0), 0.0))
    return outer(tile), b, c


def mobility(t, alpha):
    return jnp.where(t != 0.0, 1.0 / (1.0 + 9.0 * alpha), 0.0)


def resistance_of(mobile):
    return jnp.where(mobile > 0.0, 1.0 / mobile, WALL)


def weight(t, diag):
    return jnp.where(is_active(t) & (diag >= 0.5), 1.0 / diag, 0.0)


def with_coupling(scale, k):
    return scale / (1.0 + k * scale)


def edge_planes(own, edge, inner, far):
    low, lower_far = (edge, inner) if edge == 0 else (inner, far)
    k_edge, stays_edge, passes_edge = between(own, low)
    k_far, stays_far, passes_far = between(own, lower_far)
    if edge == 0:
        edge_flux, inner_flux = stays_edge, passes_edge + stays_far
    else:
        edge_flux, inner_flux = passes_edge, stays_edge + passes_far

    def sums(p, flux_len, k_len):
        flux, sum_y, sum_z, _, _ = in_plane_terms(own, p, own.resist(p))
        t = own.get("t", p)
        source = own.get("lp", p) + jnp.where(t != 0.0, own.get("la", p) + (flux_len + flux), 0.0)
        return source, weight(t, 0.5 + (k_len + sum_y + sum_z))

    source_in, weight_in = sums(inner, inner_flux, k_edge + k_far)
    carried = k_edge * (source_in * weight_in)
    source, scale = sums(edge, edge_flux, k_edge)
    return mobility(own.get("t", edge), own.get("al", edge)), own.get("la", edge), source, scale, carried


def early_kernel(al, ve, up, ct, la, lp, out):
    own = Own(al, ve, up, ct, la, lp, None)
    top = PLANES - 1
    planes = edge_planes(own, top, top - 1, top - 2) + (own.get("c0", top), own.get("m0", top))
    for i, plane in enumerate(planes):
        out[pl.ds(i * ROWS, ROWS), :] = plane[:ROWS]


def early(*args):
    return pl.pallas_call(
        early_kernel,
        out_shape=jax.ShapeDtypeStruct((EARLY_ROWS, NZ), jnp.float32),
        compiler_params=PARAMS,
        name="early",
    )(*args)


def end_rows(plane):
    return jnp.where(sublanes((HALO, NZ)) == 0, plane[:HALO], plane[ROWS - HALO : ROWS])


def slab_kernel(al, ve, up, ct, la, lp, prev, nxt, halo, down, upper):
    fill_halo(prev, nxt, halo)
    own = Own(al, ve, up, ct, la, lp, halo)
    top = PLANES - 1
    planes = edge_planes(own, 0, 1, 2)
    mobile, lam, source, scale, _ = planes
    for i, plane in enumerate(planes):
        down[pl.ds(i * ROWS, ROWS), :] = plane[:ROWS]
    down[pl.ds(5 * ROWS, HALO), :] = pack_trio(mobile[ROWS:], source[ROWS:], scale[ROWS:])
    down[pl.ds(5 * ROWS + HALO, HALO), :] = lam[ROWS:]
    mobile, lam, source, scale, carried = edge_planes(own, top, top - 1, top - 2)
    tiles = [
        pack_trio(mobile[ROWS:], source[ROWS:], scale[ROWS:]),
        pack_pair(lam[ROWS:], own.get("c0", top)[ROWS:]),
        own.get("m0", top)[ROWS:],
        pack_trio(end_rows(source), end_rows(scale), end_rows(carried)),
    ]
    for i, tile in enumerate(tiles):
        upper[pl.ds(i * HALO, HALO), :] = tile


def slabs(*args):
    return pl.pallas_call(
        slab_kernel,
        out_shape=[
            jax.ShapeDtypeStruct((len(FIELDS), PLANES, HALO, NZ), jnp.float32),
            jax.ShapeDtypeStruct((DOWN_ROWS, NZ), jnp.float32),
            jax.ShapeDtypeStruct((UP_ROWS, NZ), jnp.float32),
        ],
        compiler_params=PARAMS,
        cost_estimate=pl.CostEstimate(flops=SLAB_FLOPS, bytes_accessed=SLAB_BYTES, transcendentals=0),
        name="slabs",
    )(*args)


def joined(planes, halos):
    return [jnp.concatenate([a, b], axis=0) for a, b in zip(planes, halos)]


def rows_of(ref, count):
    return [ref[pl.ds(i * ROWS, ROWS), :] for i in range(count)]


def tiles_of(ref, planes, count):
    return [ref[pl.ds(planes * ROWS + i * HALO, HALO), :] for i in range(count)]


def read_above(ref):
    first, second = tiles_of(ref, 5, 2)
    mobile, source, scale = unpack_trio(first)
    return joined(rows_of(ref, 5), [mobile, outer(second), source, scale, jnp.zeros_like(first)])


def with_ends(plane, ends):
    row = sublanes((HALO, NZ))
    first = jnp.where(row == 0, ends, plane[:HALO])
    last = jnp.where(row == HALO - 1, ends, plane[ROWS - HALO :])
    return jnp.concatenate([first, plane[HALO : ROWS - HALO], last], axis=0)


def read_below(raw, ref):
    first, second, third, fourth = tiles_of(ref, 0, 4)
    mobile, source, scale = unpack_trio(first)
    lam, speed = unpack_pair(second)
    planes = rows_of(raw, 7)
    for i, ends in enumerate(unpack_trio(fourth)):
        planes[2 + i] = with_ends(planes[2 + i], ends)
    return joined(planes, [mobile, lam, source, scale, jnp.zeros_like(first), speed, outer(third)])


def sweep(i, x, source, scale, kl, ky, kz):
    mid = x(i)
    k_y, k_z = ky(i), kz(i)
    beside = k_y * up_y(mid) + down_y(k_y) * down_y(mid)
    beside = beside + (k_z * up_z(mid) + down_z(k_z) * down_z(mid))
    if i < PLANES:
        beside = beside + kl(i) * x(i + 1)
    if i >= 0:
        beside = beside + kl(i - 1) * x(i - 1)
    return (source(i) + beside) * scale(i)


def inner_kernel(al, ve, up, ct, la, lp, halo, grad, press, column, edges, source, scale, kl, ky, kz, first, second):
    own = Own(al, ve, up, ct, la, lp, halo)
    top = PLANES - 1
    incoming = 0.0
    for p in range(PLANES):
        r, t, lam = own.resist(p), own.get("t", p), own.get("la", p)
        flux, sum_y, sum_z, k_y, k_z = in_plane_terms(own, p, r)
        k_sum = sum_y + sum_z
        if p < top:
            k, stays, passes = between(own, p)
            kl[p] = k
            flux = flux + stays
            k_sum = k_sum + k
        if p > 0:
            flux = flux + incoming
            k_sum = k_sum + kl[p - 1]
        incoming = passes
        total = jnp.where(t != 0.0, lam + flux, 0.0)
        grad[p] = total[:ROWS]
        ky[p], kz[p] = k_y, k_z
        source[p] = own.get("lp", p) + total
        scale[p] = weight(t, 0.5 + k_sum)
        first[p] = source[p] * scale[p]
    kl[top] = jnp.zeros((EXT, NZ), jnp.float32)
    kept = (own.resist(0), own.get("la", 0), own.resist(top), own.get("la", top), own.get("c0", top), own.get("m0", top))
    for i, plane in enumerate(kept):
        edges[i] = plane

    def at(ref):
        return lambda i: ref[i]

    coefficients = [at(ref) for ref in (source, scale, kl, ky, kz)]
    zero = jnp.zeros((EXT, NZ), jnp.float32)
    for p in range(PLANES):
        second[p] = sweep(p, at(first), *coefficients) if 2 <= p < PLANES - 2 else zero
    total = jnp.zeros((ROWS, NZ), jnp.float32)
    for p in range(PLANES):
        if 3 <= p < PLANES - 3:
            x = sweep(p, at(second), *coefficients)[:ROWS]
            total = total + jnp.where(ct[p] == 2, la[p] + x, 0.0)
        else:
            x = zero[:ROWS]
        press[p] = x
    column[...] = total


def inner(args, halo):
    field = jax.ShapeDtypeStruct((PLANES, ROWS, NZ), jnp.float32)
    wide = jax.ShapeDtypeStruct((PLANES, EXT, NZ), jnp.float32)
    kept = jax.ShapeDtypeStruct((6, EXT, NZ), jnp.float32)
    return pl.pallas_call(
        inner_kernel,
        out_shape=[field, field, jax.ShapeDtypeStruct((ROWS, NZ), jnp.float32), kept] + [wide] * 7,
        compiler_params=PARAMS,
        cost_estimate=pl.CostEstimate(flops=20_000_000, bytes_accessed=6_000_000, transcendentals=0),
        name="inner",
    )(*args, halo)


def relax_kernel(
    ct, la, ow, raw, below, above, grad_in, press_in, column_in, edges, source, scale, kl, ky, kz, first, second,
    grad, press, sums,
):
    top = PLANES - 1
    s_b, la_b, src_b, w_b, carried_b, c_b, m_b = read_below(raw, below)
    s_a, la_a, src_a, w_a, carried_a = read_above(above)
    r_b, r_a = resistance_of(s_b), resistance_of(s_a)
    r_0, la_0, r_7, la_7, c_7, m_7 = (edges[i] for i in range(6))
    through, k_b = coupling(r_b, r_0)
    stays_b, passes_b = split_flux(through, c_b, m_b, la_b, la_0)
    through, k_a = coupling(r_7, r_a)
    stays_a, passes_a = split_flux(through, c_7, m_7, la_7, la_a)
    _, ky_b, _, kz_b = in_plane(r_b)
    _, ky_a, _, kz_a = in_plane(r_a)

    def at(ref, changed):
        return lambda i: changed[i] if i in changed else ref[i]

    sources = {-1: src_b + stays_b, 0: source[0] + passes_b, top: source[top] + stays_a, PLANES: src_a + passes_a}
    scales = {-1: with_coupling(w_b, k_b), 0: with_coupling(scale[0], k_b)}
    scales |= {top: with_coupling(scale[top], k_a), PLANES: with_coupling(w_a, k_a)}
    x = at(first, {i: sources[i] * scales[i] for i in sources})
    sources[-1] = sources[-1] + carried_b
    sources[PLANES] = sources[PLANES] + carried_a
    coefficients = (
        at(source, sources),
        at(scale, scales),
        at(kl, {-1: k_b, top: k_a}),
        at(ky, {-1: ky_b, PLANES: ky_a}),
        at(kz, {-1: kz_b, PLANES: kz_a}),
    )
    done = range(2, PLANES - 2)
    x = at(second, {i: sweep(i, x, *coefficients) for i in range(-1, PLANES + 1) if i not in done})
    done = range(3, PLANES - 3)
    column = column_in[...]
    for p in range(PLANES):
        if p in done:
            press[p] = press_in[p]
        else:
            value = sweep(p, x, *coefficients)[:ROWS]
            press[p] = value
            column = column + jnp.where(ct[p] == 2, la[p] + value, 0.0)
        grad[p] = grad_in[p]
    grad[0] = grad_in[0] + passes_b[:ROWS]
    grad[top] = grad_in[top] + stays_a[:ROWS]
    owner = ow[...]
    parts = []
    for port in range(PORTS):
        mine = jnp.where(owner == port, column, 0.0)
        mine = mine[:, :128] + mine[:, 128:]
        parts.append(jnp.sum(mine, axis=0, keepdims=True))
    table = jnp.sum(jnp.concatenate(parts, axis=0), axis=1, keepdims=True)
    diagonal = lanes((PORTS, 128)) == sublanes((PORTS, 128))
    line = jnp.sum(jnp.where(diagonal, table, 0.0), axis=0, keepdims=True)
    sums[...] = jnp.broadcast_to(line, sums.shape)


def relax(celltype, lam, owner, raw, below, above, inside):
    field = jax.ShapeDtypeStruct((PLANES, ROWS, NZ), jnp.float32)
    return pl.pallas_call(
        relax_kernel,
        out_shape=[field, field, jax.ShapeDtypeStruct((size_of(FIRST), 128), jnp.float32)],
        compiler_params=PARAMS,
        name="relax",
    )(celltype, lam, owner, raw, below, above, *inside)


def faces_kernel(al, ve, up, ct, la, lp, halo, above, out):
    own = Own(al, ve, up, ct, la, lp, halo)
    mobile, la_a = read_above(above)[:2]
    r_a = resistance_of(mobile)
    al_a = (r_a - 1.0) / 9.0

    def write(axis, p, through, speed, donor, lam, lam_next, alpha, alpha_next):
        face = jnp.where(through, speed * (lam_next - lam), 0.0)
        out[axis, p] = (face * jnp.where(donor != 0.0, alpha, alpha_next))[:ROWS]

    for p in range(PLANES):
        r, alpha, lam = own.resist(p), own.get("al", p), own.get("la", p)
        inner = p < PLANES - 1
        r_next = own.resist(p + 1) if inner else r_a
        alpha_next = own.get("al", p + 1) if inner else al_a
        lam_next = own.get("la", p + 1) if inner else la_a
        through, _ = coupling(r, r_next)
        write(0, p, through, own.get("c0", p), own.get("m0", p), lam, lam_next, alpha, alpha_next)
        through, _ = coupling(r, up_y(r))
        write(1, p, through, own.get("c1", p), own.get("m1", p), lam, up_y(lam), alpha, up_y(alpha))
        through, _ = coupling(r, up_z(r))
        through = through & (lanes(r.shape) < NZ - 1)
        write(2, p, through, own.get("c2", p), own.get("m2", p), lam, up_z(lam), alpha, up_z(alpha))


def faces(alpha, velocity, upwind, celltype, lam, lam_press, halo, above):
    return pl.pallas_call(
        faces_kernel,
        out_shape=jax.ShapeDtypeStruct((3, PLANES, ROWS, NZ), jnp.float32),
        compiler_params=PARAMS,
        cost_estimate=pl.CostEstimate(flops=5_000_000, bytes_accessed=4_000_000, transcendentals=0),
        name="faces",
    )(alpha, velocity, upwind, celltype, lam, lam_press, halo, above)


def total_over(copies, axes):
    return jnp.sum(lax.all_to_all(copies, axes, 0, 0, tiled=True), axis=0)


def body(alpha, velocity, upwind, celltype, owner, lam_alpha, lam_press):
    args = (alpha, velocity, upwind, celltype, lam_alpha, lam_press)
    to_next, to_prev = strips(*args)
    prev = shift(to_next, XS, 1)
    nxt = shift(to_prev, XS, -1)
    raw = shift(early(*args), LEN, 1)
    halo, down, upper = slabs(*args, prev, nxt)
    above = shift(down, LEN, -1)
    below = shift(upper, LEN, 1)
    inside = inner(args, halo)
    grad_alpha, press, sums = relax(celltype, lam_alpha, owner, raw, below, above, inside)
    grad_velocity = faces(*args, halo, above)
    sums = total_over(sums, FIRST)
    sums = total_over(jnp.broadcast_to(sums[None], (size_of(SECOND), 128)), SECOND)
    cells = math.prod(alpha.shape) * size_of(LEN + XS)
    return (grad_alpha, grad_velocity, press, sums[:PORTS] / math.sqrt(cells))


def solution(mesh):
    parts = Mesh(mesh.devices.reshape(tuple(SIZES.values())), tuple(SIZES))
    field = P(LEN, XS, None)
    faces_spec = P(None, LEN, XS, None)
    in_specs = (field, faces_spec, faces_spec, field, P(XS, None), field, field)
    out_specs = (field, faces_spec, field, P())
    return jax.shard_map(body, mesh=parts, in_specs=in_specs, out_specs=out_specs, check_vma=False)
```

```python
import functools
import math

import jax
import jax.numpy as jnp
from jax import lax
from jax.experimental import pallas as pl
from jax.experimental.pallas import tpu as pltpu
from jax.sharding import Mesh
from jax.sharding import PartitionSpec as P

SWEEPS = 2
PORTS = 16
LEN = ("x", "z", "yh")
XS = ("yl", "c")
FIRST = ("x", "yh", "yl")
SECOND = ("z", "c")
SIZES = {"x": 4, "z": 12, "yh": 2, "yl": 4, "c": 2}
PLANES = 8
ROWS = 32
HALO = 8
EXT = ROWS + HALO
NZ = 256
WALL = 1e30
VMEM_LIMIT = 16 * 2**20
SLAB_FLOPS = 20_000_000
SLAB_BYTES = 40_000_000
STRIP = (("t", 3), ("al", 3), ("la", 3), ("lp", 2), ("c0", 2), ("m0", 2), ("c1", 3), ("m1", 2), ("c2", 2), ("m2", 2))
FIELDS = [name for name, _ in STRIP]
EARLY_ROWS = 7 * ROWS
DOWN_ROWS = 5 * ROWS + 2 * HALO
UP_ROWS = 4 * HALO
PARAMS = pltpu.CompilerParams(vmem_limit_bytes=VMEM_LIMIT)


def size_of(axes):
    return math.prod(SIZES[a] for a in axes)


def shift(x, axes, by):
    count = size_of(axes)
    pairs = [(i, i + by) for i in range(count) if 0 <= i + by < count]
    return lax.ppermute(x, axes, pairs)


def swap(x, axes, first):
    pairs = [(i, i + 1) for i in range(first, size_of(axes) - 1, 2)]
    return lax.ppermute(x, axes, pairs + [(j, i) for i, j in pairs])


def is_lower():
    return lax.axis_index("c") == 0


def up_y(x):
    return pltpu.roll(x, EXT - 1, 0)


def down_y(x):
    return pltpu.roll(x, 1, 0)


def up_z(x):
    return pltpu.roll(x, NZ - 1, 1)


def down_z(x):
    return pltpu.roll(x, 1, 1)


def resistance(t, alpha):
    return jnp.where(t != 0.0, 1.0 + 9.0 * alpha, WALL)


def coupling(low, high):
    both = low + high
    through = both < 0.5 * WALL
    return through, jnp.where(through, 2.0 / both, 0.0)


def is_active(t):
    return jnp.abs(t) == 1.0


def split_flux(through, speed, donor, low, high):
    face = jnp.where(through, speed * (high - low), 0.0)
    stays = face * donor
    return stays, face - stays


def lanes(shape):
    return lax.broadcasted_iota(jnp.int32, shape, 1)


def sublanes(shape):
    return lax.broadcasted_iota(jnp.int32, shape, 0)


def strip_kernel(al, ve, up, ct, la, lp, in_chip, off_chip, *scratch):
    sem = scratch[-1]
    last, first = scratch[:6], scratch[6:12]
    copies = []
    for kept, start in ((last, ROWS - HALO), (first, 0)):
        for source, target in zip((al, ve, up, ct, la, lp), kept):
            rows = pl.ds(start, HALO)
            window = source.at[:, rows, :] if len(source.shape) == 3 else source.at[:, :, rows, :]
            copies.append(pltpu.make_async_copy(window, target, sem.at[len(copies)]))
            copies[-1].start()
    for copy in copies:
        copy.wait()
    def value_of(name, count, kept, is_last):
        al_k, ve_k, up_k, ct_k, la_k, lp_k = kept
        rows = pl.ds(HALO - count if is_last else 0, count)
        if name == "t":
            return ct_k[:, rows, :].astype(jnp.float32) - 1.0
        if name in ("al", "la", "lp"):
            return {"al": al_k, "la": la_k, "lp": lp_k}[name][:, rows, :]
        if name[0] == "m":
            return up_k[int(name[1]), :, rows, :].astype(jnp.float32)
        value = 0.4 * ve_k[int(name[1]), :, rows, :]
        if name == "c1" and is_last:
            donor = up_k[1, :, rows, :].astype(jnp.float32)
            row = lax.broadcasted_iota(jnp.int32, value.shape, 1)
            value = jnp.where(row == 0, value * (1.0 - donor), value)
        return value

    at = 0
    for name, count in STRIP:
        to_next = value_of(name, count, last, True)
        to_prev = value_of(name, count, first, False)
        in_chip[:, pl.ds(at, count), :] = jnp.where(is_lower(), to_next, to_prev)
        off_chip[:, pl.ds(at, count), :] = jnp.where(is_lower(), to_prev, to_next)
        at += count


def strips(*args):
    message = jax.ShapeDtypeStruct((PLANES, 24, NZ), jnp.float32)
    kept = [pltpu.VMEM(x.shape[:-2] + (HALO, NZ), x.dtype) for x in args]
    return pl.pallas_call(
        strip_kernel,
        in_specs=[pl.BlockSpec(memory_space=pltpu.HBM)] * 6,
        out_shape=[message, message],
        scratch_shapes=kept + kept + [pltpu.SemaphoreType.DMA((12,))],
        compiler_params=PARAMS,
        name="strips",
    )(*(pltpu.with_memory_space_constraint(x, pltpu.HBM) for x in args))


class Own:
    def __init__(self, al, ve, up, ct, la, lp, halo):
        self.refs = (al, ve, up, ct, la, lp, halo)

    def get(self, name, p):
        al, ve, up, ct, la, lp, halo = self.refs
        if name == "t":
            own = ct[p].astype(jnp.float32) - 1.0
        elif name in ("al", "la", "lp"):
            own = {"al": al, "la": la, "lp": lp}[name][p]
        elif name[0] == "c":
            own = 0.4 * ve[int(name[1]), p]
        else:
            own = up[int(name[1]), p].astype(jnp.float32)
        tile = jnp.zeros((HALO, NZ), jnp.float32) if halo is None else halo[FIELDS.index(name), p]
        return jnp.concatenate([own, tile], axis=0)

    def resist(self, p):
        return resistance(self.get("t", p), self.get("al", p))


def in_plane(r):
    through_y, ky = coupling(r, up_y(r))
    through_z, kz = coupling(r, up_z(r))
    inside = lanes(r.shape) < NZ - 1
    return through_y, ky, through_z & inside, jnp.where(inside, kz, 0.0)


def in_plane_terms(own, p, r):
    through_y, ky, through_z, kz = in_plane(r)
    la = own.get("la", p)
    stays, passes = split_flux(through_y, own.get("c1", p), own.get("m1", p), la, up_y(la))
    flux = stays + down_y(passes)
    stays, passes = split_flux(through_z, own.get("c2", p), own.get("m2", p), la, up_z(la))
    flux = flux + (stays + down_z(passes))
    return flux, ky + down_y(ky), kz + down_z(kz), ky, kz


def between(own, p):
    through, k = coupling(own.resist(p), own.resist(p + 1))
    stays, passes = split_flux(through, own.get("c0", p), own.get("m0", p), own.get("la", p), own.get("la", p + 1))
    return k, stays, passes


def fill_halo(in_chip, off_chip, halo):
    prev = jnp.where(is_lower(), off_chip[...], in_chip[...])
    nxt = jnp.where(is_lower(), in_chip[...], off_chip[...])
    at = 0
    halo[...] = jnp.zeros(halo.shape, jnp.float32)
    for f, (_, count) in enumerate(STRIP):
        halo[f, :, pl.ds(0, count), :] = nxt[:, at : at + count, :]
        halo[f, :, pl.ds(HALO - count, count), :] = prev[:, at : at + count, :]
        at += count


def pack_pair(a, b):
    row = sublanes(a.shape)
    low = (row == 2) | (row == 3)
    high = (row == 4) | (row == 5)
    return jnp.where(low, pltpu.roll(b, 2, 0), jnp.where(high, pltpu.roll(b, HALO - 2, 0), a))


def pack_trio(a, b, c):
    row = sublanes(a.shape)
    out = jnp.where(row == 2, pltpu.roll(b, 2, 0), a)
    out = jnp.where(row == 5, pltpu.roll(b, HALO - 2, 0), out)
    out = jnp.where(row == 3, pltpu.roll(c, 3, 0), out)
    return jnp.where(row == 4, pltpu.roll(c, HALO - 3, 0), out)


def outer(a):
    row = sublanes(a.shape)
    return jnp.where((row < 2) | (row > 5), a, 0.0)


def unpack_pair(tile):
    row = sublanes(tile.shape)
    b = jnp.where(row < 2, pltpu.roll(tile, HALO - 2, 0), jnp.where(row > 5, pltpu.roll(tile, 2, 0), 0.0))
    return outer(tile), b


def unpack_trio(tile):
    row = sublanes(tile.shape)
    b = jnp.where(row == 0, pltpu.roll(tile, HALO - 2, 0), jnp.where(row == 7, pltpu.roll(tile, 2, 0), 0.0))
    c = jnp.where(row == 0, pltpu.roll(tile, HALO - 3, 0), jnp.where(row == 7, pltpu.roll(tile, 3, 0), 0.0))
    return outer(tile), b, c


def mobility(t, alpha):
    return jnp.where(t != 0.0, 1.0 / (1.0 + 9.0 * alpha), 0.0)


def resistance_of(mobile):
    return jnp.where(mobile > 0.0, 1.0 / mobile, WALL)


def weight(t, diag):
    return jnp.where(is_active(t) & (diag >= 0.5), 1.0 / diag, 0.0)


def with_coupling(scale, k):
    return scale / (1.0 + k * scale)


def edge_planes(own, edge, inner, far):
    low, lower_far = (edge, inner) if edge == 0 else (inner, far)
    k_edge, stays_edge, passes_edge = between(own, low)
    k_far, stays_far, passes_far = between(own, lower_far)
    if edge == 0:
        edge_flux, inner_flux = stays_edge, passes_edge + stays_far
    else:
        edge_flux, inner_flux = passes_edge, stays_edge + passes_far

    def sums(p, flux_len, k_len):
        flux, sum_y, sum_z, _, _ = in_plane_terms(own, p, own.resist(p))
        t = own.get("t", p)
        source = own.get("lp", p) + jnp.where(t != 0.0, own.get("la", p) + (flux_len + flux), 0.0)
        return source, weight(t, 0.5 + (k_len + sum_y + sum_z))

    source_in, weight_in = sums(inner, inner_flux, k_edge + k_far)
    carried = k_edge * (source_in * weight_in)
    source, scale = sums(edge, edge_flux, k_edge)
    return mobility(own.get("t", edge), own.get("al", edge)), own.get("la", edge), source, scale, carried


def early_kernel(al, ve, up, ct, la, lp, out):
    own = Own(al, ve, up, ct, la, lp, None)
    top = PLANES - 1
    planes = edge_planes(own, top, top - 1, top - 2) + (own.get("c0", top), own.get("m0", top))
    for i, plane in enumerate(planes):
        out[pl.ds(i * ROWS, ROWS), :] = plane[:ROWS]


def early(*args):
    return pl.pallas_call(
        early_kernel,
        out_shape=jax.ShapeDtypeStruct((EARLY_ROWS, NZ), jnp.float32),
        compiler_params=PARAMS,
        name="early",
    )(*args)


def end_rows(plane):
    return jnp.where(sublanes((HALO, NZ)) == 0, plane[:HALO], plane[ROWS - HALO : ROWS])


def slab_kernel(al, ve, up, ct, la, lp, in_chip, off_chip, halo, down, upper):
    fill_halo(in_chip, off_chip, halo)
    own = Own(al, ve, up, ct, la, lp, halo)
    top = PLANES - 1
    planes = edge_planes(own, 0, 1, 2)
    mobile, lam, source, scale, _ = planes
    for i, plane in enumerate(planes):
        down[pl.ds(i * ROWS, ROWS), :] = plane[:ROWS]
    down[pl.ds(5 * ROWS, HALO), :] = pack_trio(mobile[ROWS:], source[ROWS:], scale[ROWS:])
    down[pl.ds(5 * ROWS + HALO, HALO), :] = lam[ROWS:]
    mobile, lam, source, scale, carried = edge_planes(own, top, top - 1, top - 2)
    tiles = [
        pack_trio(mobile[ROWS:], source[ROWS:], scale[ROWS:]),
        pack_pair(lam[ROWS:], own.get("c0", top)[ROWS:]),
        own.get("m0", top)[ROWS:],
        pack_trio(end_rows(source), end_rows(scale), end_rows(carried)),
    ]
    for i, tile in enumerate(tiles):
        upper[pl.ds(i * HALO, HALO), :] = tile


def slabs(*args):
    return pl.pallas_call(
        slab_kernel,
        out_shape=[
            jax.ShapeDtypeStruct((len(FIELDS), PLANES, HALO, NZ), jnp.float32),
            jax.ShapeDtypeStruct((DOWN_ROWS, NZ), jnp.float32),
            jax.ShapeDtypeStruct((UP_ROWS, NZ), jnp.float32),
        ],
        compiler_params=PARAMS,
        cost_estimate=pl.CostEstimate(flops=SLAB_FLOPS, bytes_accessed=SLAB_BYTES, transcendentals=0),
        name="slabs",
    )(*args)


def joined(planes, halos):
    return [jnp.concatenate([a, b], axis=0) for a, b in zip(planes, halos)]


def rows_of(ref, count):
    return [ref[pl.ds(i * ROWS, ROWS), :] for i in range(count)]


def tiles_of(ref, planes, count):
    return [ref[pl.ds(planes * ROWS + i * HALO, HALO), :] for i in range(count)]


def read_above(ref):
    first, second = tiles_of(ref, 5, 2)
    mobile, source, scale = unpack_trio(first)
    return joined(rows_of(ref, 5), [mobile, outer(second), source, scale, jnp.zeros_like(first)])


def with_ends(plane, ends):
    row = sublanes((HALO, NZ))
    first = jnp.where(row == 0, ends, plane[:HALO])
    last = jnp.where(row == HALO - 1, ends, plane[ROWS - HALO :])
    return jnp.concatenate([first, plane[HALO : ROWS - HALO], last], axis=0)


def read_below(raw, ref):
    first, second, third, fourth = tiles_of(ref, 0, 4)
    mobile, source, scale = unpack_trio(first)
    lam, speed = unpack_pair(second)
    planes = rows_of(raw, 7)
    for i, ends in enumerate(unpack_trio(fourth)):
        planes[2 + i] = with_ends(planes[2 + i], ends)
    return joined(planes, [mobile, lam, source, scale, jnp.zeros_like(first), speed, outer(third)])


def sweep(i, x, source, scale, kl, ky, kz):
    mid = x(i)
    k_y, k_z = ky(i), kz(i)
    beside = k_y * up_y(mid) + down_y(k_y) * down_y(mid)
    beside = beside + (k_z * up_z(mid) + down_z(k_z) * down_z(mid))
    if i < PLANES:
        beside = beside + kl(i) * x(i + 1)
    if i >= 0:
        beside = beside + kl(i - 1) * x(i - 1)
    return (source(i) + beside) * scale(i)


def inner_kernel(al, ve, up, ct, la, lp, halo, grad, press, column, edges, source, scale, kl, ky, kz, first, second):
    own = Own(al, ve, up, ct, la, lp, halo)
    top = PLANES - 1
    incoming = 0.0
    for p in range(PLANES):
        r, t, lam = own.resist(p), own.get("t", p), own.get("la", p)
        flux, sum_y, sum_z, k_y, k_z = in_plane_terms(own, p, r)
        k_sum = sum_y + sum_z
        if p < top:
            k, stays, passes = between(own, p)
            kl[p] = k
            flux = flux + stays
            k_sum = k_sum + k
        if p > 0:
            flux = flux + incoming
            k_sum = k_sum + kl[p - 1]
        incoming = passes
        total = jnp.where(t != 0.0, lam + flux, 0.0)
        grad[p] = total[:ROWS]
        ky[p], kz[p] = k_y, k_z
        source[p] = own.get("lp", p) + total
        scale[p] = weight(t, 0.5 + k_sum)
        first[p] = source[p] * scale[p]
    kl[top] = jnp.zeros((EXT, NZ), jnp.float32)
    kept = (own.resist(0), own.get("la", 0), own.resist(top), own.get("la", top), own.get("c0", top), own.get("m0", top))
    for i, plane in enumerate(kept):
        edges[i] = plane

    def at(ref):
        return lambda i: ref[i]

    coefficients = [at(ref) for ref in (source, scale, kl, ky, kz)]
    zero = jnp.zeros((EXT, NZ), jnp.float32)
    for p in range(PLANES):
        second[p] = sweep(p, at(first), *coefficients) if 2 <= p < PLANES - 2 else zero
    total = jnp.zeros((ROWS, NZ), jnp.float32)
    for p in range(PLANES):
        if 3 <= p < PLANES - 3:
            x = sweep(p, at(second), *coefficients)[:ROWS]
            total = total + jnp.where(ct[p] == 2, la[p] + x, 0.0)
        else:
            x = zero[:ROWS]
        press[p] = x
    column[...] = total


def inner(args, halo):
    field = jax.ShapeDtypeStruct((PLANES, ROWS, NZ), jnp.float32)
    wide = jax.ShapeDtypeStruct((PLANES, EXT, NZ), jnp.float32)
    kept = jax.ShapeDtypeStruct((6, EXT, NZ), jnp.float32)
    return pl.pallas_call(
        inner_kernel,
        out_shape=[field, field, jax.ShapeDtypeStruct((ROWS, NZ), jnp.float32), kept] + [wide] * 7,
        compiler_params=PARAMS,
        cost_estimate=pl.CostEstimate(flops=20_000_000, bytes_accessed=6_000_000, transcendentals=0),
        name="inner",
    )(*args, halo)


def relax_kernel(
    ct, la, ow, raw, below, above, grad_in, press_in, column_in, edges, source, scale, kl, ky, kz, first, second,
    grad, press, sums,
):
    top = PLANES - 1
    s_b, la_b, src_b, w_b, carried_b, c_b, m_b = read_below(raw, below)
    s_a, la_a, src_a, w_a, carried_a = read_above(above)
    r_b, r_a = resistance_of(s_b), resistance_of(s_a)
    r_0, la_0, r_7, la_7, c_7, m_7 = (edges[i] for i in range(6))
    through, k_b = coupling(r_b, r_0)
    stays_b, passes_b = split_flux(through, c_b, m_b, la_b, la_0)
    through, k_a = coupling(r_7, r_a)
    stays_a, passes_a = split_flux(through, c_7, m_7, la_7, la_a)
    _, ky_b, _, kz_b = in_plane(r_b)
    _, ky_a, _, kz_a = in_plane(r_a)

    def at(ref, changed):
        return lambda i: changed[i] if i in changed else ref[i]

    sources = {-1: src_b + stays_b, 0: source[0] + passes_b, top: source[top] + stays_a, PLANES: src_a + passes_a}
    scales = {-1: with_coupling(w_b, k_b), 0: with_coupling(scale[0], k_b)}
    scales |= {top: with_coupling(scale[top], k_a), PLANES: with_coupling(w_a, k_a)}
    x = at(first, {i: sources[i] * scales[i] for i in sources})
    sources[-1] = sources[-1] + carried_b
    sources[PLANES] = sources[PLANES] + carried_a
    coefficients = (
        at(source, sources),
        at(scale, scales),
        at(kl, {-1: k_b, top: k_a}),
        at(ky, {-1: ky_b, PLANES: ky_a}),
        at(kz, {-1: kz_b, PLANES: kz_a}),
    )
    done = range(2, PLANES - 2)
    x = at(second, {i: sweep(i, x, *coefficients) for i in range(-1, PLANES + 1) if i not in done})
    done = range(3, PLANES - 3)
    column = column_in[...]
    for p in range(PLANES):
        if p in done:
            press[p] = press_in[p]
        else:
            value = sweep(p, x, *coefficients)[:ROWS]
            press[p] = value
            column = column + jnp.where(ct[p] == 2, la[p] + value, 0.0)
        grad[p] = grad_in[p]
    grad[0] = grad_in[0] + passes_b[:ROWS]
    grad[top] = grad_in[top] + stays_a[:ROWS]
    owner = ow[...]
    parts = []
    for port in range(PORTS):
        mine = jnp.where(owner == port, column, 0.0)
        mine = mine[:, :128] + mine[:, 128:]
        parts.append(jnp.sum(mine, axis=0, keepdims=True))
    table = jnp.sum(jnp.concatenate(parts, axis=0), axis=1, keepdims=True)
    diagonal = lanes((PORTS, 128)) == sublanes((PORTS, 128))
    line = jnp.sum(jnp.where(diagonal, table, 0.0), axis=0, keepdims=True)
    sums[...] = jnp.broadcast_to(line, sums.shape)


def relax(celltype, lam, owner, raw, below, above, inside):
    field = jax.ShapeDtypeStruct((PLANES, ROWS, NZ), jnp.float32)
    return pl.pallas_call(
        relax_kernel,
        out_shape=[field, field, jax.ShapeDtypeStruct((size_of(FIRST), 128), jnp.float32)],
        compiler_params=PARAMS,
        name="relax",
    )(celltype, lam, owner, raw, below, above, *inside)


def faces_kernel(al, ve, up, ct, la, lp, halo, above, out):
    own = Own(al, ve, up, ct, la, lp, halo)
    mobile, la_a = read_above(above)[:2]
    r_a = resistance_of(mobile)
    al_a = (r_a - 1.0) / 9.0

    def write(axis, p, through, speed, donor, lam, lam_next, alpha, alpha_next):
        face = jnp.where(through, speed * (lam_next - lam), 0.0)
        out[axis, p] = (face * jnp.where(donor != 0.0, alpha, alpha_next))[:ROWS]

    for p in range(PLANES):
        r, alpha, lam = own.resist(p), own.get("al", p), own.get("la", p)
        inner = p < PLANES - 1
        r_next = own.resist(p + 1) if inner else r_a
        alpha_next = own.get("al", p + 1) if inner else al_a
        lam_next = own.get("la", p + 1) if inner else la_a
        through, _ = coupling(r, r_next)
        write(0, p, through, own.get("c0", p), own.get("m0", p), lam, lam_next, alpha, alpha_next)
        through, _ = coupling(r, up_y(r))
        write(1, p, through, own.get("c1", p), own.get("m1", p), lam, up_y(lam), alpha, up_y(alpha))
        through, _ = coupling(r, up_z(r))
        through = through & (lanes(r.shape) < NZ - 1)
        write(2, p, through, own.get("c2", p), own.get("m2", p), lam, up_z(lam), alpha, up_z(alpha))


def faces(alpha, velocity, upwind, celltype, lam, lam_press, halo, above):
    return pl.pallas_call(
        faces_kernel,
        out_shape=jax.ShapeDtypeStruct((3, PLANES, ROWS, NZ), jnp.float32),
        compiler_params=PARAMS,
        cost_estimate=pl.CostEstimate(flops=5_000_000, bytes_accessed=4_000_000, transcendentals=0),
        name="faces",
    )(alpha, velocity, upwind, celltype, lam, lam_press, halo, above)


def total_over(copies, axes):
    return jnp.sum(lax.all_to_all(copies, axes, 0, 0, tiled=True), axis=0)


def body(alpha, velocity, upwind, celltype, owner, lam_alpha, lam_press):
    args = (alpha, velocity, upwind, celltype, lam_alpha, lam_press)
    in_chip, off_chip = strips(*args)
    in_chip = swap(in_chip, XS, 0)
    off_chip = swap(off_chip, XS, 1)
    raw = shift(early(*args), LEN, 1)
    halo, down, upper = slabs(*args, in_chip, off_chip)
    above = shift(down, LEN, -1)
    below = shift(upper, LEN, 1)
    inside = inner(args, halo)
    grad_alpha, press, sums = relax(celltype, lam_alpha, owner, raw, below, above, inside)
    grad_velocity = faces(*args, halo, above)
    sums = total_over(sums, FIRST)
    sums = total_over(jnp.broadcast_to(sums[None], (size_of(SECOND), 128)), SECOND)
    cells = math.prod(alpha.shape) * size_of(LEN + XS)
    return (grad_alpha, grad_velocity, press, sums[:PORTS] / math.sqrt(cells))


def solution(mesh):
    parts = Mesh(mesh.devices.reshape(tuple(SIZES.values())), tuple(SIZES))
    field = P(LEN, XS, None)
    faces_spec = P(None, LEN, XS, None)
    in_specs = (field, faces_spec, faces_spec, field, P(XS, None), field, field)
    out_specs = (field, faces_spec, field, P())
    return jax.shard_map(body, mesh=parts, in_specs=in_specs, out_specs=out_specs, check_vma=False)
```

```python
import functools
import math

import jax
import jax.numpy as jnp
from jax import lax
from jax.experimental import pallas as pl
from jax.experimental.pallas import tpu as pltpu
from jax.sharding import Mesh
from jax.sharding import PartitionSpec as P

SWEEPS = 2
PORTS = 16
LEN = ("x", "z", "yh")
XS = ("yl", "c")
FIRST = ("z", "c")
SECOND = ("x", "yh", "yl")
SIZES = {"x": 4, "z": 12, "yh": 2, "yl": 4, "c": 2}
PLANES = 8
ROWS = 32
HALO = 8
EXT = ROWS + HALO
NZ = 256
WALL = 1e30
VMEM_LIMIT = 16 * 2**20
SLAB_FLOPS = 20_000_000
SLAB_BYTES = 40_000_000
STRIP = (("t", 3), ("al", 3), ("la", 3), ("lp", 2), ("c0", 2), ("m0", 2), ("c1", 3), ("m1", 2), ("c2", 2), ("m2", 2))
FIELDS = [name for name, _ in STRIP]
EARLY_ROWS = 7 * ROWS
DOWN_ROWS = 5 * ROWS + 2 * HALO
UP_ROWS = 4 * HALO
PARAMS = pltpu.CompilerParams(vmem_limit_bytes=VMEM_LIMIT)


def size_of(axes):
    return math.prod(SIZES[a] for a in axes)


def shift(x, axes, by):
    count = size_of(axes)
    pairs = [(i, i + by) for i in range(count) if 0 <= i + by < count]
    return lax.ppermute(x, axes, pairs)


def swap(x, axes, first):
    pairs = [(i, i + 1) for i in range(first, size_of(axes) - 1, 2)]
    return lax.ppermute(x, axes, pairs + [(j, i) for i, j in pairs])


def is_lower():
    return lax.axis_index("c") == 0


def up_y(x):
    return pltpu.roll(x, EXT - 1, 0)


def down_y(x):
    return pltpu.roll(x, 1, 0)


def up_z(x):
    return pltpu.roll(x, NZ - 1, 1)


def down_z(x):
    return pltpu.roll(x, 1, 1)


def resistance(t, alpha):
    return jnp.where(t != 0.0, 1.0 + 9.0 * alpha, WALL)


def coupling(low, high):
    both = low + high
    through = both < 0.5 * WALL
    return through, jnp.where(through, 2.0 / both, 0.0)


def is_active(t):
    return jnp.abs(t) == 1.0


def split_flux(through, speed, donor, low, high):
    face = jnp.where(through, speed * (high - low), 0.0)
    stays = face * donor
    return stays, face - stays


def lanes(shape):
    return lax.broadcasted_iota(jnp.int32, shape, 1)


def sublanes(shape):
    return lax.broadcasted_iota(jnp.int32, shape, 0)


def strip_kernel(al, ve, up, ct, la, lp, in_chip, off_chip, *scratch):
    sem = scratch[-1]
    last, first = scratch[:6], scratch[6:12]
    copies = []
    for kept, start in ((last, ROWS - HALO), (first, 0)):
        for source, target in zip((al, ve, up, ct, la, lp), kept):
            rows = pl.ds(start, HALO)
            window = source.at[:, rows, :] if len(source.shape) == 3 else source.at[:, :, rows, :]
            copies.append(pltpu.make_async_copy(window, target, sem.at[len(copies)]))
            copies[-1].start()
    for copy in copies:
        copy.wait()
    def value_of(name, count, kept, is_last):
        al_k, ve_k, up_k, ct_k, la_k, lp_k = kept
        rows = pl.ds(HALO - count if is_last else 0, count)
        if name == "t":
            return ct_k[:, rows, :].astype(jnp.float32) - 1.0
        if name in ("al", "la", "lp"):
            return {"al": al_k, "la": la_k, "lp": lp_k}[name][:, rows, :]
        if name[0] == "m":
            return up_k[int(name[1]), :, rows, :].astype(jnp.float32)
        value = 0.4 * ve_k[int(name[1]), :, rows, :]
        if name == "c1" and is_last:
            donor = up_k[1, :, rows, :].astype(jnp.float32)
            row = lax.broadcasted_iota(jnp.int32, value.shape, 1)
            value = jnp.where(row == 0, value * (1.0 - donor), value)
        return value

    at = 0
    for name, count in STRIP:
        to_next = value_of(name, count, last, True)
        to_prev = value_of(name, count, first, False)
        in_chip[:, pl.ds(at, count), :] = jnp.where(is_lower(), to_next, to_prev)
        off_chip[:, pl.ds(at, count), :] = jnp.where(is_lower(), to_prev, to_next)
        at += count


def strips(*args):
    message = jax.ShapeDtypeStruct((PLANES, 24, NZ), jnp.float32)
    kept = [pltpu.VMEM(x.shape[:-2] + (HALO, NZ), x.dtype) for x in args]
    return pl.pallas_call(
        strip_kernel,
        in_specs=[pl.BlockSpec(memory_space=pltpu.HBM)] * 6,
        out_shape=[message, message],
        scratch_shapes=kept + kept + [pltpu.SemaphoreType.DMA((12,))],
        compiler_params=PARAMS,
        name="strips",
    )(*(pltpu.with_memory_space_constraint(x, pltpu.HBM) for x in args))


class Own:
    def __init__(self, al, ve, up, ct, la, lp, halo):
        self.refs = (al, ve, up, ct, la, lp, halo)

    def get(self, name, p):
        al, ve, up, ct, la, lp, halo = self.refs
        if name == "t":
            own = ct[p].astype(jnp.float32) - 1.0
        elif name in ("al", "la", "lp"):
            own = {"al": al, "la": la, "lp": lp}[name][p]
        elif name[0] == "c":
            own = 0.4 * ve[int(name[1]), p]
        else:
            own = up[int(name[1]), p].astype(jnp.float32)
        tile = jnp.zeros((HALO, NZ), jnp.float32) if halo is None else halo[FIELDS.index(name), p]
        return jnp.concatenate([own, tile], axis=0)

    def resist(self, p):
        return resistance(self.get("t", p), self.get("al", p))


def in_plane(r):
    through_y, ky = coupling(r, up_y(r))
    through_z, kz = coupling(r, up_z(r))
    inside = lanes(r.shape) < NZ - 1
    return through_y, ky, through_z & inside, jnp.where(inside, kz, 0.0)


def in_plane_terms(own, p, r):
    through_y, ky, through_z, kz = in_plane(r)
    la = own.get("la", p)
    stays, passes = split_flux(through_y, own.get("c1", p), own.get("m1", p), la, up_y(la))
    flux = stays + down_y(passes)
    stays, passes = split_flux(through_z, own.get("c2", p), own.get("m2", p), la, up_z(la))
    flux = flux + (stays + down_z(passes))
    return flux, ky + down_y(ky), kz + down_z(kz), ky, kz


def between(own, p):
    through, k = coupling(own.resist(p), own.resist(p + 1))
    stays, passes = split_flux(through, own.get("c0", p), own.get("m0", p), own.get("la", p), own.get("la", p + 1))
    return k, stays, passes


def fill_halo(in_chip, off_chip, halo):
    prev = jnp.where(is_lower(), off_chip[...], in_chip[...])
    nxt = jnp.where(is_lower(), in_chip[...], off_chip[...])
    at = 0
    halo[...] = jnp.zeros(halo.shape, jnp.float32)
    for f, (_, count) in enumerate(STRIP):
        halo[f, :, pl.ds(0, count), :] = nxt[:, at : at + count, :]
        halo[f, :, pl.ds(HALO - count, count), :] = prev[:, at : at + count, :]
        at += count


def pack_pair(a, b):
    row = sublanes(a.shape)
    low = (row == 2) | (row == 3)
    high = (row == 4) | (row == 5)
    return jnp.where(low, pltpu.roll(b, 2, 0), jnp.where(high, pltpu.roll(b, HALO - 2, 0), a))


def pack_trio(a, b, c):
    row = sublanes(a.shape)
    out = jnp.where(row == 2, pltpu.roll(b, 2, 0), a)
    out = jnp.where(row == 5, pltpu.roll(b, HALO - 2, 0), out)
    out = jnp.where(row == 3, pltpu.roll(c, 3, 0), out)
    return jnp.where(row == 4, pltpu.roll(c, HALO - 3, 0), out)


def outer(a):
    row = sublanes(a.shape)
    return jnp.where((row < 2) | (row > 5), a, 0.0)


def unpack_pair(tile):
    row = sublanes(tile.shape)
    b = jnp.where(row < 2, pltpu.roll(tile, HALO - 2, 0), jnp.where(row > 5, pltpu.roll(tile, 2, 0), 0.0))
    return outer(tile), b


def unpack_trio(tile):
    row = sublanes(tile.shape)
    b = jnp.where(row == 0, pltpu.roll(tile, HALO - 2, 0), jnp.where(row == 7, pltpu.roll(tile, 2, 0), 0.0))
    c = jnp.where(row == 0, pltpu.roll(tile, HALO - 3, 0), jnp.where(row == 7, pltpu.roll(tile, 3, 0), 0.0))
    return outer(tile), b, c


def mobility(t, alpha):
    return jnp.where(t != 0.0, 1.0 / (1.0 + 9.0 * alpha), 0.0)


def resistance_of(mobile):
    return jnp.where(mobile > 0.0, 1.0 / mobile, WALL)


def weight(t, diag):
    return jnp.where(is_active(t) & (diag >= 0.5), 1.0 / diag, 0.0)


def with_coupling(scale, k):
    return scale / (1.0 + k * scale)


def edge_planes(own, edge, inner, far):
    low, lower_far = (edge, inner) if edge == 0 else (inner, far)
    k_edge, stays_edge, passes_edge = between(own, low)
    k_far, stays_far, passes_far = between(own, lower_far)
    if edge == 0:
        edge_flux, inner_flux = stays_edge, passes_edge + stays_far
    else:
        edge_flux, inner_flux = passes_edge, stays_edge + passes_far

    def sums(p, flux_len, k_len):
        flux, sum_y, sum_z, _, _ = in_plane_terms(own, p, own.resist(p))
        t = own.get("t", p)
        source = own.get("lp", p) + jnp.where(t != 0.0, own.get("la", p) + (flux_len + flux), 0.0)
        return source, weight(t, 0.5 + (k_len + sum_y + sum_z))

    source_in, weight_in = sums(inner, inner_flux, k_edge + k_far)
    carried = k_edge * (source_in * weight_in)
    source, scale = sums(edge, edge_flux, k_edge)
    return mobility(own.get("t", edge), own.get("al", edge)), own.get("la", edge), source, scale, carried


def early_kernel(al, ve, up, ct, la, lp, out):
    own = Own(al, ve, up, ct, la, lp, None)
    top = PLANES - 1
    planes = edge_planes(own, top, top - 1, top - 2) + (own.get("c0", top), own.get("m0", top))
    for i, plane in enumerate(planes):
        out[pl.ds(i * ROWS, ROWS), :] = plane[:ROWS]


def early(*args):
    return pl.pallas_call(
        early_kernel,
        out_shape=jax.ShapeDtypeStruct((EARLY_ROWS, NZ), jnp.float32),
        compiler_params=PARAMS,
        name="early",
    )(*args)


def end_rows(plane):
    return jnp.where(sublanes((HALO, NZ)) == 0, plane[:HALO], plane[ROWS - HALO : ROWS])


def slab_kernel(al, ve, up, ct, la, lp, in_chip, off_chip, halo, down, upper):
    fill_halo(in_chip, off_chip, halo)
    own = Own(al, ve, up, ct, la, lp, halo)
    top = PLANES - 1
    planes = edge_planes(own, 0, 1, 2)
    mobile, lam, source, scale, _ = planes
    for i, plane in enumerate(planes):
        down[pl.ds(i * ROWS, ROWS), :] = plane[:ROWS]
    down[pl.ds(5 * ROWS, HALO), :] = pack_trio(mobile[ROWS:], source[ROWS:], scale[ROWS:])
    down[pl.ds(5 * ROWS + HALO, HALO), :] = lam[ROWS:]
    mobile, lam, source, scale, carried = edge_planes(own, top, top - 1, top - 2)
    tiles = [
        pack_trio(mobile[ROWS:], source[ROWS:], scale[ROWS:]),
        pack_pair(lam[ROWS:], own.get("c0", top)[ROWS:]),
        own.get("m0", top)[ROWS:],
        pack_trio(end_rows(source), end_rows(scale), end_rows(carried)),
    ]
    for i, tile in enumerate(tiles):
        upper[pl.ds(i * HALO, HALO), :] = tile


def slabs(*args):
    return pl.pallas_call(
        slab_kernel,
        out_shape=[
            jax.ShapeDtypeStruct((len(FIELDS), PLANES, HALO, NZ), jnp.float32),
            jax.ShapeDtypeStruct((DOWN_ROWS, NZ), jnp.float32),
            jax.ShapeDtypeStruct((UP_ROWS, NZ), jnp.float32),
        ],
        compiler_params=PARAMS,
        cost_estimate=pl.CostEstimate(flops=SLAB_FLOPS, bytes_accessed=SLAB_BYTES, transcendentals=0),
        name="slabs",
    )(*args)


def joined(planes, halos):
    return [jnp.concatenate([a, b], axis=0) for a, b in zip(planes, halos)]


def rows_of(ref, count):
    return [ref[pl.ds(i * ROWS, ROWS), :] for i in range(count)]


def tiles_of(ref, planes, count):
    return [ref[pl.ds(planes * ROWS + i * HALO, HALO), :] for i in range(count)]


def read_above(ref):
    first, second = tiles_of(ref, 5, 2)
    mobile, source, scale = unpack_trio(first)
    return joined(rows_of(ref, 5), [mobile, outer(second), source, scale, jnp.zeros_like(first)])


def with_ends(plane, ends):
    row = sublanes((HALO, NZ))
    first = jnp.where(row == 0, ends, plane[:HALO])
    last = jnp.where(row == HALO - 1, ends, plane[ROWS - HALO :])
    return jnp.concatenate([first, plane[HALO : ROWS - HALO], last], axis=0)


def read_below(raw, ref):
    first, second, third, fourth = tiles_of(ref, 0, 4)
    mobile, source, scale = unpack_trio(first)
    lam, speed = unpack_pair(second)
    planes = rows_of(raw, 7)
    for i, ends in enumerate(unpack_trio(fourth)):
        planes[2 + i] = with_ends(planes[2 + i], ends)
    return joined(planes, [mobile, lam, source, scale, jnp.zeros_like(first), speed, outer(third)])


def sweep(i, x, source, scale, kl, ky, kz):
    mid = x(i)
    k_y, k_z = ky(i), kz(i)
    beside = k_y * up_y(mid) + down_y(k_y) * down_y(mid)
    beside = beside + (k_z * up_z(mid) + down_z(k_z) * down_z(mid))
    if i < PLANES:
        beside = beside + kl(i) * x(i + 1)
    if i >= 0:
        beside = beside + kl(i - 1) * x(i - 1)
    return (source(i) + beside) * scale(i)


def inner_kernel(al, ve, up, ct, la, lp, halo, grad, press, column, edges, source, scale, kl, ky, kz, first, second):
    own = Own(al, ve, up, ct, la, lp, halo)
    top = PLANES - 1
    incoming = 0.0
    for p in range(PLANES):
        r, t, lam = own.resist(p), own.get("t", p), own.get("la", p)
        flux, sum_y, sum_z, k_y, k_z = in_plane_terms(own, p, r)
        k_sum = sum_y + sum_z
        if p < top:
            k, stays, passes = between(own, p)
            kl[p] = k
            flux = flux + stays
            k_sum = k_sum + k
        if p > 0:
            flux = flux + incoming
            k_sum = k_sum + kl[p - 1]
        incoming = passes
        total = jnp.where(t != 0.0, lam + flux, 0.0)
        grad[p] = total[:ROWS]
        ky[p], kz[p] = k_y, k_z
        source[p] = own.get("lp", p) + total
        scale[p] = weight(t, 0.5 + k_sum)
        first[p] = source[p] * scale[p]
    kl[top] = jnp.zeros((EXT, NZ), jnp.float32)
    kept = (own.resist(0), own.get("la", 0), own.resist(top), own.get("la", top), own.get("c0", top), own.get("m0", top))
    for i, plane in enumerate(kept):
        edges[i] = plane

    def at(ref):
        return lambda i: ref[i]

    coefficients = [at(ref) for ref in (source, scale, kl, ky, kz)]
    zero = jnp.zeros((EXT, NZ), jnp.float32)
    for p in range(PLANES):
        second[p] = sweep(p, at(first), *coefficients) if 2 <= p < PLANES - 2 else zero
    total = jnp.zeros((ROWS, NZ), jnp.float32)
    for p in range(PLANES):
        if 3 <= p < PLANES - 3:
            x = sweep(p, at(second), *coefficients)[:ROWS]
            total = total + jnp.where(ct[p] == 2, la[p] + x, 0.0)
        else:
            x = zero[:ROWS]
        press[p] = x
    column[...] = total


def inner(args, halo):
    field = jax.ShapeDtypeStruct((PLANES, ROWS, NZ), jnp.float32)
    wide = jax.ShapeDtypeStruct((PLANES, EXT, NZ), jnp.float32)
    kept = jax.ShapeDtypeStruct((6, EXT, NZ), jnp.float32)
    return pl.pallas_call(
        inner_kernel,
        out_shape=[field, field, jax.ShapeDtypeStruct((ROWS, NZ), jnp.float32), kept] + [wide] * 7,
        compiler_params=PARAMS,
        cost_estimate=pl.CostEstimate(flops=20_000_000, bytes_accessed=6_000_000, transcendentals=0),
        name="inner",
    )(*args, halo)


def relax_kernel(
    ct, la, ow, raw, below, above, grad_in, press_in, column_in, edges, source, scale, kl, ky, kz, first, second,
    grad, press, sums,
):
    top = PLANES - 1
    s_b, la_b, src_b, w_b, carried_b, c_b, m_b = read_below(raw, below)
    s_a, la_a, src_a, w_a, carried_a = read_above(above)
    r_b, r_a = resistance_of(s_b), resistance_of(s_a)
    r_0, la_0, r_7, la_7, c_7, m_7 = (edges[i] for i in range(6))
    through, k_b = coupling(r_b, r_0)
    stays_b, passes_b = split_flux(through, c_b, m_b, la_b, la_0)
    through, k_a = coupling(r_7, r_a)
    stays_a, passes_a = split_flux(through, c_7, m_7, la_7, la_a)
    _, ky_b, _, kz_b = in_plane(r_b)
    _, ky_a, _, kz_a = in_plane(r_a)

    def at(ref, changed):
        return lambda i: changed[i] if i in changed else ref[i]

    sources = {-1: src_b + stays_b, 0: source[0] + passes_b, top: source[top] + stays_a, PLANES: src_a + passes_a}
    scales = {-1: with_coupling(w_b, k_b), 0: with_coupling(scale[0], k_b)}
    scales |= {top: with_coupling(scale[top], k_a), PLANES: with_coupling(w_a, k_a)}
    x = at(first, {i: sources[i] * scales[i] for i in sources})
    sources[-1] = sources[-1] + carried_b
    sources[PLANES] = sources[PLANES] + carried_a
    coefficients = (
        at(source, sources),
        at(scale, scales),
        at(kl, {-1: k_b, top: k_a}),
        at(ky, {-1: ky_b, PLANES: ky_a}),
        at(kz, {-1: kz_b, PLANES: kz_a}),
    )
    done = range(2, PLANES - 2)
    x = at(second, {i: sweep(i, x, *coefficients) for i in range(-1, PLANES + 1) if i not in done})
    done = range(3, PLANES - 3)
    column = column_in[...]
    for p in range(PLANES):
        if p in done:
            press[p] = press_in[p]
        else:
            value = sweep(p, x, *coefficients)[:ROWS]
            press[p] = value
            column = column + jnp.where(ct[p] == 2, la[p] + value, 0.0)
        grad[p] = grad_in[p]
    grad[0] = grad_in[0] + passes_b[:ROWS]
    grad[top] = grad_in[top] + stays_a[:ROWS]
    owner = ow[...]
    parts = []
    for port in range(PORTS):
        mine = jnp.where(owner == port, column, 0.0)
        mine = mine[:, :128] + mine[:, 128:]
        parts.append(jnp.sum(mine, axis=0, keepdims=True))
    table = jnp.sum(jnp.concatenate(parts, axis=0), axis=1, keepdims=True)
    diagonal = lanes((PORTS, 128)) == sublanes((PORTS, 128))
    line = jnp.sum(jnp.where(diagonal, table, 0.0), axis=0, keepdims=True)
    sums[...] = jnp.broadcast_to(line, sums.shape)


def relax(celltype, lam, owner, raw, below, above, inside):
    field = jax.ShapeDtypeStruct((PLANES, ROWS, NZ), jnp.float32)
    return pl.pallas_call(
        relax_kernel,
        out_shape=[field, field, jax.ShapeDtypeStruct((size_of(FIRST), 128), jnp.float32)],
        compiler_params=PARAMS,
        name="relax",
    )(celltype, lam, owner, raw, below, above, *inside)


def faces_kernel(al, ve, up, ct, la, lp, halo, above, out):
    own = Own(al, ve, up, ct, la, lp, halo)
    mobile, la_a = read_above(above)[:2]
    r_a = resistance_of(mobile)
    al_a = (r_a - 1.0) / 9.0

    def write(axis, p, through, speed, donor, lam, lam_next, alpha, alpha_next):
        face = jnp.where(through, speed * (lam_next - lam), 0.0)
        out[axis, p] = (face * jnp.where(donor != 0.0, alpha, alpha_next))[:ROWS]

    for p in range(PLANES):
        r, alpha, lam = own.resist(p), own.get("al", p), own.get("la", p)
        inner = p < PLANES - 1
        r_next = own.resist(p + 1) if inner else r_a
        alpha_next = own.get("al", p + 1) if inner else al_a
        lam_next = own.get("la", p + 1) if inner else la_a
        through, _ = coupling(r, r_next)
        write(0, p, through, own.get("c0", p), own.get("m0", p), lam, lam_next, alpha, alpha_next)
        through, _ = coupling(r, up_y(r))
        write(1, p, through, own.get("c1", p), own.get("m1", p), lam, up_y(lam), alpha, up_y(alpha))
        through, _ = coupling(r, up_z(r))
        through = through & (lanes(r.shape) < NZ - 1)
        write(2, p, through, own.get("c2", p), own.get("m2", p), lam, up_z(lam), alpha, up_z(alpha))


def faces(alpha, velocity, upwind, celltype, lam, lam_press, halo, above):
    return pl.pallas_call(
        faces_kernel,
        out_shape=jax.ShapeDtypeStruct((3, PLANES, ROWS, NZ), jnp.float32),
        compiler_params=PARAMS,
        cost_estimate=pl.CostEstimate(flops=5_000_000, bytes_accessed=4_000_000, transcendentals=0),
        name="faces",
    )(alpha, velocity, upwind, celltype, lam, lam_press, halo, above)


def total_over(copies, axes):
    return jnp.sum(lax.all_to_all(copies, axes, 0, 0, tiled=True), axis=0)


def body(alpha, velocity, upwind, celltype, owner, lam_alpha, lam_press):
    args = (alpha, velocity, upwind, celltype, lam_alpha, lam_press)
    in_chip, off_chip = strips(*args)
    in_chip = swap(in_chip, XS, 0)
    off_chip = swap(off_chip, XS, 1)
    raw = shift(early(*args), LEN, 1)
    halo, down, upper = slabs(*args, in_chip, off_chip)
    above = shift(down, LEN, -1)
    below = shift(upper, LEN, 1)
    inside = inner(args, halo)
    grad_alpha, press, sums = relax(celltype, lam_alpha, owner, raw, below, above, inside)
    grad_velocity = faces(*args, halo, above)
    sums = total_over(sums, FIRST)
    sums = total_over(jnp.broadcast_to(sums[None], (size_of(SECOND), 128)), SECOND)
    cells = math.prod(alpha.shape) * size_of(LEN + XS)
    return (grad_alpha, grad_velocity, press, sums[:PORTS] / math.sqrt(cells))


def solution(mesh):
    parts = Mesh(mesh.devices.reshape(tuple(SIZES.values())), tuple(SIZES))
    field = P(LEN, XS, None)
    faces_spec = P(None, LEN, XS, None)
    in_specs = (field, faces_spec, faces_spec, field, P(XS, None), field, field)
    out_specs = (field, faces_spec, field, P())
    return jax.shard_map(body, mesh=parts, in_specs=in_specs, out_specs=out_specs, check_vma=False)
```

```python
import functools
import math

import jax
import jax.numpy as jnp
from jax import lax
from jax.experimental import pallas as pl
from jax.experimental.pallas import tpu as pltpu
from jax.sharding import Mesh
from jax.sharding import PartitionSpec as P

SWEEPS = 2
PORTS = 16
LEN = ("x", "z", "yh")
XS = ("yl", "c")
FIRST = ("z", "c")
SECOND = ("x", "yh", "yl")
SIZES = {"x": 4, "z": 12, "yh": 2, "yl": 4, "c": 2}
PLANES = 8
ROWS = 32
HALO = 8
EXT = ROWS + HALO
NZ = 256
WALL = 1e30
VMEM_LIMIT = 16 * 2**20
SLAB_FLOPS = 20_000_000
SLAB_BYTES = 40_000_000
STRIP = (("t", 3), ("al", 3), ("la", 3), ("lp", 2), ("c0", 2), ("m0", 2), ("c1", 3), ("m1", 2), ("c2", 2), ("m2", 2))
FIELDS = [name for name, _ in STRIP]
EARLY_ROWS = 7 * ROWS
DOWN_ROWS = 5 * ROWS + 2 * HALO
UP_ROWS = 4 * HALO
PARAMS = pltpu.CompilerParams(vmem_limit_bytes=VMEM_LIMIT)


def size_of(axes):
    return math.prod(SIZES[a] for a in axes)


def shift(x, axes, by):
    count = size_of(axes)
    pairs = [(i, i + by) for i in range(count) if 0 <= i + by < count]
    return lax.ppermute(x, axes, pairs)


def swap(x, axes, first):
    pairs = [(i, i + 1) for i in range(first, size_of(axes) - 1, 2)]
    return lax.ppermute(x, axes, pairs + [(j, i) for i, j in pairs])


def is_lower():
    return lax.axis_index("c") == 0


def up_y(x):
    return pltpu.roll(x, EXT - 1, 0)


def down_y(x):
    return pltpu.roll(x, 1, 0)


def up_z(x):
    return pltpu.roll(x, NZ - 1, 1)


def down_z(x):
    return pltpu.roll(x, 1, 1)


def resistance(t, alpha):
    return jnp.where(t != 0.0, 1.0 + 9.0 * alpha, WALL)


def coupling(low, high):
    both = low + high
    through = both < 0.5 * WALL
    return through, jnp.where(through, 2.0 / both, 0.0)


def is_active(t):
    return jnp.abs(t) == 1.0


def split_flux(through, speed, donor, low, high):
    face = jnp.where(through, speed * (high - low), 0.0)
    stays = face * donor
    return stays, face - stays


def lanes(shape):
    return lax.broadcasted_iota(jnp.int32, shape, 1)


def sublanes(shape):
    return lax.broadcasted_iota(jnp.int32, shape, 0)


def strip_kernel(al, ve, up, ct, la, lp, off_chip, in_chip, *scratch):
    sem = scratch[-1]
    last, first = scratch[:6], scratch[6:12]
    copies = []
    for kept, start in ((last, ROWS - HALO), (first, 0)):
        for source, target in zip((al, ve, up, ct, la, lp), kept):
            rows = pl.ds(start, HALO)
            window = source.at[:, rows, :] if len(source.shape) == 3 else source.at[:, :, rows, :]
            copies.append(pltpu.make_async_copy(window, target, sem.at[len(copies)]))
            copies[-1].start()
    for copy in copies:
        copy.wait()
    def value_of(name, count, kept, is_last):
        al_k, ve_k, up_k, ct_k, la_k, lp_k = kept
        rows = pl.ds(HALO - count if is_last else 0, count)
        if name == "t":
            return ct_k[:, rows, :].astype(jnp.float32) - 1.0
        if name in ("al", "la", "lp"):
            return {"al": al_k, "la": la_k, "lp": lp_k}[name][:, rows, :]
        if name[0] == "m":
            return up_k[int(name[1]), :, rows, :].astype(jnp.float32)
        value = 0.4 * ve_k[int(name[1]), :, rows, :]
        if name == "c1" and is_last:
            donor = up_k[1, :, rows, :].astype(jnp.float32)
            row = lax.broadcasted_iota(jnp.int32, value.shape, 1)
            value = jnp.where(row == 0, value * (1.0 - donor), value)
        return value

    at = 0
    for name, count in STRIP:
        to_next = value_of(name, count, last, True)
        to_prev = value_of(name, count, first, False)
        in_chip[:, pl.ds(at, count), :] = jnp.where(is_lower(), to_next, to_prev)
        off_chip[:, pl.ds(at, count), :] = jnp.where(is_lower(), to_prev, to_next)
        at += count


def strips(*args):
    message = jax.ShapeDtypeStruct((PLANES, 24, NZ), jnp.float32)
    kept = [pltpu.VMEM(x.shape[:-2] + (HALO, NZ), x.dtype) for x in args]
    return pl.pallas_call(
        strip_kernel,
        in_specs=[pl.BlockSpec(memory_space=pltpu.HBM)] * 6,
        out_shape=[message, message],
        scratch_shapes=kept + kept + [pltpu.SemaphoreType.DMA((12,))],
        compiler_params=PARAMS,
        name="strips",
    )(*(pltpu.with_memory_space_constraint(x, pltpu.HBM) for x in args))


class Own:
    def __init__(self, al, ve, up, ct, la, lp, halo):
        self.refs = (al, ve, up, ct, la, lp, halo)

    def get(self, name, p):
        al, ve, up, ct, la, lp, halo = self.refs
        if name == "t":
            own = ct[p].astype(jnp.float32) - 1.0
        elif name in ("al", "la", "lp"):
            own = {"al": al, "la": la, "lp": lp}[name][p]
        elif name[0] == "c":
            own = 0.4 * ve[int(name[1]), p]
        else:
            own = up[int(name[1]), p].astype(jnp.float32)
        tile = jnp.zeros((HALO, NZ), jnp.float32) if halo is None else halo[FIELDS.index(name), p]
        return jnp.concatenate([own, tile], axis=0)

    def resist(self, p):
        return resistance(self.get("t", p), self.get("al", p))


def in_plane(r):
    through_y, ky = coupling(r, up_y(r))
    through_z, kz = coupling(r, up_z(r))
    inside = lanes(r.shape) < NZ - 1
    return through_y, ky, through_z & inside, jnp.where(inside, kz, 0.0)


def in_plane_terms(own, p, r):
    through_y, ky, through_z, kz = in_plane(r)
    la = own.get("la", p)
    stays, passes = split_flux(through_y, own.get("c1", p), own.get("m1", p), la, up_y(la))
    flux = stays + down_y(passes)
    stays, passes = split_flux(through_z, own.get("c2", p), own.get("m2", p), la, up_z(la))
    flux = flux + (stays + down_z(passes))
    return flux, ky + down_y(ky), kz + down_z(kz), ky, kz


def between(own, p):
    through, k = coupling(own.resist(p), own.resist(p + 1))
    stays, passes = split_flux(through, own.get("c0", p), own.get("m0", p), own.get("la", p), own.get("la", p + 1))
    return k, stays, passes


def fill_halo(in_chip, off_chip, halo):
    prev = jnp.where(is_lower(), off_chip[...], in_chip[...])
    nxt = jnp.where(is_lower(), in_chip[...], off_chip[...])
    at = 0
    halo[...] = jnp.zeros(halo.shape, jnp.float32)
    for f, (_, count) in enumerate(STRIP):
        halo[f, :, pl.ds(0, count), :] = nxt[:, at : at + count, :]
        halo[f, :, pl.ds(HALO - count, count), :] = prev[:, at : at + count, :]
        at += count


def pack_pair(a, b):
    row = sublanes(a.shape)
    low = (row == 2) | (row == 3)
    high = (row == 4) | (row == 5)
    return jnp.where(low, pltpu.roll(b, 2, 0), jnp.where(high, pltpu.roll(b, HALO - 2, 0), a))


def pack_trio(a, b, c):
    row = sublanes(a.shape)
    out = jnp.where(row == 2, pltpu.roll(b, 2, 0), a)
    out = jnp.where(row == 5, pltpu.roll(b, HALO - 2, 0), out)
    out = jnp.where(row == 3, pltpu.roll(c, 3, 0), out)
    return jnp.where(row == 4, pltpu.roll(c, HALO - 3, 0), out)


def outer(a):
    row = sublanes(a.shape)
    return jnp.where((row < 2) | (row > 5), a, 0.0)


def unpack_pair(tile):
    row = sublanes(tile.shape)
    b = jnp.where(row < 2, pltpu.roll(tile, HALO - 2, 0), jnp.where(row > 5, pltpu.roll(tile, 2, 0), 0.0))
    return outer(tile), b


def unpack_trio(tile):
    row = sublanes(tile.shape)
    b = jnp.where(row == 0, pltpu.roll(tile, HALO - 2, 0), jnp.where(row == 7, pltpu.roll(tile, 2, 0), 0.0))
    c = jnp.where(row == 0, pltpu.roll(tile, HALO - 3, 0), jnp.where(row == 7, pltpu.roll(tile, 3, 0), 0.0))
    return outer(tile), b, c


def mobility(t, alpha):
    return jnp.where(t != 0.0, 1.0 / (1.0 + 9.0 * alpha), 0.0)


def resistance_of(mobile):
    return jnp.where(mobile > 0.0, 1.0 / mobile, WALL)


def weight(t, diag):
    return jnp.where(is_active(t) & (diag >= 0.5), 1.0 / diag, 0.0)


def with_coupling(scale, k):
    return scale / (1.0 + k * scale)


def edge_planes(own, edge, inner, far):
    low, lower_far = (edge, inner) if edge == 0 else (inner, far)
    k_edge, stays_edge, passes_edge = between(own, low)
    k_far, stays_far, passes_far = between(own, lower_far)
    if edge == 0:
        edge_flux, inner_flux = stays_edge, passes_edge + stays_far
    else:
        edge_flux, inner_flux = passes_edge, stays_edge + passes_far

    def sums(p, flux_len, k_len):
        flux, sum_y, sum_z, _, _ = in_plane_terms(own, p, own.resist(p))
        t = own.get("t", p)
        source = own.get("lp", p) + jnp.where(t != 0.0, own.get("la", p) + (flux_len + flux), 0.0)
        return source, weight(t, 0.5 + (k_len + sum_y + sum_z))

    source_in, weight_in = sums(inner, inner_flux, k_edge + k_far)
    carried = k_edge * (source_in * weight_in)
    source, scale = sums(edge, edge_flux, k_edge)
    return mobility(own.get("t", edge), own.get("al", edge)), own.get("la", edge), source, scale, carried


def early_kernel(al, ve, up, ct, la, lp, out):
    own = Own(al, ve, up, ct, la, lp, None)
    top = PLANES - 1
    planes = edge_planes(own, top, top - 1, top - 2) + (own.get("c0", top), own.get("m0", top))
    for i, plane in enumerate(planes):
        out[pl.ds(i * ROWS, ROWS), :] = plane[:ROWS]


def early(*args):
    return pl.pallas_call(
        early_kernel,
        out_shape=jax.ShapeDtypeStruct((EARLY_ROWS, NZ), jnp.float32),
        compiler_params=PARAMS,
        name="early",
    )(*args)


def end_rows(plane):
    return jnp.where(sublanes((HALO, NZ)) == 0, plane[:HALO], plane[ROWS - HALO : ROWS])


def slab_kernel(al, ve, up, ct, la, lp, off_chip, in_chip, halo, down, upper):
    fill_halo(in_chip, off_chip, halo)
    own = Own(al, ve, up, ct, la, lp, halo)
    top = PLANES - 1
    planes = edge_planes(own, 0, 1, 2)
    mobile, lam, source, scale, _ = planes
    for i, plane in enumerate(planes):
        down[pl.ds(i * ROWS, ROWS), :] = plane[:ROWS]
    down[pl.ds(5 * ROWS, HALO), :] = pack_trio(mobile[ROWS:], source[ROWS:], scale[ROWS:])
    down[pl.ds(5 * ROWS + HALO, HALO), :] = lam[ROWS:]
    mobile, lam, source, scale, carried = edge_planes(own, top, top - 1, top - 2)
    tiles = [
        pack_trio(mobile[ROWS:], source[ROWS:], scale[ROWS:]),
        pack_pair(lam[ROWS:], own.get("c0", top)[ROWS:]),
        own.get("m0", top)[ROWS:],
        pack_trio(end_rows(source), end_rows(scale), end_rows(carried)),
    ]
    for i, tile in enumerate(tiles):
        upper[pl.ds(i * HALO, HALO), :] = tile


def slabs(*args):
    return pl.pallas_call(
        slab_kernel,
        out_shape=[
            jax.ShapeDtypeStruct((len(FIELDS), PLANES, HALO, NZ), jnp.float32),
            jax.ShapeDtypeStruct((DOWN_ROWS, NZ), jnp.float32),
            jax.ShapeDtypeStruct((UP_ROWS, NZ), jnp.float32),
        ],
        compiler_params=PARAMS,
        cost_estimate=pl.CostEstimate(flops=SLAB_FLOPS, bytes_accessed=SLAB_BYTES, transcendentals=0),
        name="slabs",
    )(*args)


def joined(planes, halos):
    return [jnp.concatenate([a, b], axis=0) for a, b in zip(planes, halos)]


def rows_of(ref, count):
    return [ref[pl.ds(i * ROWS, ROWS), :] for i in range(count)]


def tiles_of(ref, planes, count):
    return [ref[pl.ds(planes * ROWS + i * HALO, HALO), :] for i in range(count)]


def read_above(ref):
    first, second = tiles_of(ref, 5, 2)
    mobile, source, scale = unpack_trio(first)
    return joined(rows_of(ref, 5), [mobile, outer(second), source, scale, jnp.zeros_like(first)])


def with_ends(plane, ends):
    row = sublanes((HALO, NZ))
    first = jnp.where(row == 0, ends, plane[:HALO])
    last = jnp.where(row == HALO - 1, ends, plane[ROWS - HALO :])
    return jnp.concatenate([first, plane[HALO : ROWS - HALO], last], axis=0)


def read_below(raw, ref):
    first, second, third, fourth = tiles_of(ref, 0, 4)
    mobile, source, scale = unpack_trio(first)
    lam, speed = unpack_pair(second)
    planes = rows_of(raw, 7)
    for i, ends in enumerate(unpack_trio(fourth)):
        planes[2 + i] = with_ends(planes[2 + i], ends)
    return joined(planes, [mobile, lam, source, scale, jnp.zeros_like(first), speed, outer(third)])


def sweep(i, x, source, scale, kl, ky, kz):
    mid = x(i)
    k_y, k_z = ky(i), kz(i)
    beside = k_y * up_y(mid) + down_y(k_y) * down_y(mid)
    beside = beside + (k_z * up_z(mid) + down_z(k_z) * down_z(mid))
    if i < PLANES:
        beside = beside + kl(i) * x(i + 1)
    if i >= 0:
        beside = beside + kl(i - 1) * x(i - 1)
    return (source(i) + beside) * scale(i)


def inner_kernel(al, ve, up, ct, la, lp, halo, grad, press, column, edges, source, scale, kl, ky, kz, first, second):
    own = Own(al, ve, up, ct, la, lp, halo)
    top = PLANES - 1
    incoming = 0.0
    for p in range(PLANES):
        r, t, lam = own.resist(p), own.get("t", p), own.get("la", p)
        flux, sum_y, sum_z, k_y, k_z = in_plane_terms(own, p, r)
        k_sum = sum_y + sum_z
        if p < top:
            k, stays, passes = between(own, p)
            kl[p] = k
            flux = flux + stays
            k_sum = k_sum + k
        if p > 0:
            flux = flux + incoming
            k_sum = k_sum + kl[p - 1]
        incoming = passes
        total = jnp.where(t != 0.0, lam + flux, 0.0)
        grad[p] = total[:ROWS]
        ky[p], kz[p] = k_y, k_z
        source[p] = own.get("lp", p) + total
        scale[p] = weight(t, 0.5 + k_sum)
        first[p] = source[p] * scale[p]
    kl[top] = jnp.zeros((EXT, NZ), jnp.float32)
    kept = (own.resist(0), own.get("la", 0), own.resist(top), own.get("la", top), own.get("c0", top), own.get("m0", top))
    for i, plane in enumerate(kept):
        edges[i] = plane

    def at(ref):
        return lambda i: ref[i]

    coefficients = [at(ref) for ref in (source, scale, kl, ky, kz)]
    zero = jnp.zeros((EXT, NZ), jnp.float32)
    for p in range(PLANES):
        second[p] = sweep(p, at(first), *coefficients) if 2 <= p < PLANES - 2 else zero
    total = jnp.zeros((ROWS, NZ), jnp.float32)
    for p in range(PLANES):
        if 3 <= p < PLANES - 3:
            x = sweep(p, at(second), *coefficients)[:ROWS]
            total = total + jnp.where(ct[p] == 2, la[p] + x, 0.0)
        else:
            x = zero[:ROWS]
        press[p] = x
    column[...] = total


def inner(args, halo):
    field = jax.ShapeDtypeStruct((PLANES, ROWS, NZ), jnp.float32)
    wide = jax.ShapeDtypeStruct((PLANES, EXT, NZ), jnp.float32)
    kept = jax.ShapeDtypeStruct((6, EXT, NZ), jnp.float32)
    return pl.pallas_call(
        inner_kernel,
        out_shape=[field, field, jax.ShapeDtypeStruct((ROWS, NZ), jnp.float32), kept] + [wide] * 7,
        compiler_params=PARAMS,
        cost_estimate=pl.CostEstimate(flops=20_000_000, bytes_accessed=6_000_000, transcendentals=0),
        name="inner",
    )(*args, halo)


def relax_kernel(
    ct, la, ow, raw, below, above, grad_in, press_in, column_in, edges, source, scale, kl, ky, kz, first, second,
    grad, press, sums,
):
    top = PLANES - 1
    s_b, la_b, src_b, w_b, carried_b, c_b, m_b = read_below(raw, below)
    s_a, la_a, src_a, w_a, carried_a = read_above(above)
    r_b, r_a = resistance_of(s_b), resistance_of(s_a)
    r_0, la_0, r_7, la_7, c_7, m_7 = (edges[i] for i in range(6))
    through, k_b = coupling(r_b, r_0)
    stays_b, passes_b = split_flux(through, c_b, m_b, la_b, la_0)
    through, k_a = coupling(r_7, r_a)
    stays_a, passes_a = split_flux(through, c_7, m_7, la_7, la_a)
    _, ky_b, _, kz_b = in_plane(r_b)
    _, ky_a, _, kz_a = in_plane(r_a)

    def at(ref, changed):
        return lambda i: changed[i] if i in changed else ref[i]

    sources = {-1: src_b + stays_b, 0: source[0] + passes_b, top: source[top] + stays_a, PLANES: src_a + passes_a}
    scales = {-1: with_coupling(w_b, k_b), 0: with_coupling(scale[0], k_b)}
    scales |= {top: with_coupling(scale[top], k_a), PLANES: with_coupling(w_a, k_a)}
    x = at(first, {i: sources[i] * scales[i] for i in sources})
    sources[-1] = sources[-1] + carried_b
    sources[PLANES] = sources[PLANES] + carried_a
    coefficients = (
        at(source, sources),
        at(scale, scales),
        at(kl, {-1: k_b, top: k_a}),
        at(ky, {-1: ky_b, PLANES: ky_a}),
        at(kz, {-1: kz_b, PLANES: kz_a}),
    )
    done = range(2, PLANES - 2)
    x = at(second, {i: sweep(i, x, *coefficients) for i in range(-1, PLANES + 1) if i not in done})
    done = range(3, PLANES - 3)
    column = column_in[...]
    for p in range(PLANES):
        if p in done:
            press[p] = press_in[p]
        else:
            value = sweep(p, x, *coefficients)[:ROWS]
            press[p] = value
            column = column + jnp.where(ct[p] == 2, la[p] + value, 0.0)
        grad[p] = grad_in[p]
    grad[0] = grad_in[0] + passes_b[:ROWS]
    grad[top] = grad_in[top] + stays_a[:ROWS]
    owner = ow[...]
    parts = []
    for port in range(PORTS):
        mine = jnp.where(owner == port, column, 0.0)
        mine = mine[:, :128] + mine[:, 128:]
        parts.append(jnp.sum(mine, axis=0, keepdims=True))
    table = jnp.sum(jnp.concatenate(parts, axis=0), axis=1, keepdims=True)
    diagonal = lanes((PORTS, 128)) == sublanes((PORTS, 128))
    line = jnp.sum(jnp.where(diagonal, table, 0.0), axis=0, keepdims=True)
    sums[...] = jnp.broadcast_to(line, sums.shape)


def relax(celltype, lam, owner, raw, below, above, inside):
    field = jax.ShapeDtypeStruct((PLANES, ROWS, NZ), jnp.float32)
    return pl.pallas_call(
        relax_kernel,
        out_shape=[field, field, jax.ShapeDtypeStruct((size_of(FIRST), 128), jnp.float32)],
        compiler_params=PARAMS,
        name="relax",
    )(celltype, lam, owner, raw, below, above, *inside)


def faces_kernel(al, ve, up, ct, la, lp, halo, above, out):
    own = Own(al, ve, up, ct, la, lp, halo)
    mobile, la_a = read_above(above)[:2]
    r_a = resistance_of(mobile)
    al_a = (r_a - 1.0) / 9.0

    def write(axis, p, through, speed, donor, lam, lam_next, alpha, alpha_next):
        face = jnp.where(through, speed * (lam_next - lam), 0.0)
        out[axis, p] = (face * jnp.where(donor != 0.0, alpha, alpha_next))[:ROWS]

    for p in range(PLANES):
        r, alpha, lam = own.resist(p), own.get("al", p), own.get("la", p)
        inner = p < PLANES - 1
        r_next = own.resist(p + 1) if inner else r_a
        alpha_next = own.get("al", p + 1) if inner else al_a
        lam_next = own.get("la", p + 1) if inner else la_a
        through, _ = coupling(r, r_next)
        write(0, p, through, own.get("c0", p), own.get("m0", p), lam, lam_next, alpha, alpha_next)
        through, _ = coupling(r, up_y(r))
        write(1, p, through, own.get("c1", p), own.get("m1", p), lam, up_y(lam), alpha, up_y(alpha))
        through, _ = coupling(r, up_z(r))
        through = through & (lanes(r.shape) < NZ - 1)
        write(2, p, through, own.get("c2", p), own.get("m2", p), lam, up_z(lam), alpha, up_z(alpha))


def faces(alpha, velocity, upwind, celltype, lam, lam_press, halo, above):
    return pl.pallas_call(
        faces_kernel,
        out_shape=jax.ShapeDtypeStruct((3, PLANES, ROWS, NZ), jnp.float32),
        compiler_params=PARAMS,
        cost_estimate=pl.CostEstimate(flops=5_000_000, bytes_accessed=4_000_000, transcendentals=0),
        name="faces",
    )(alpha, velocity, upwind, celltype, lam, lam_press, halo, above)


def total_over(copies, axes):
    return jnp.sum(lax.all_to_all(copies, axes, 0, 0, tiled=True), axis=0)


def body(alpha, velocity, upwind, celltype, owner, lam_alpha, lam_press):
    args = (alpha, velocity, upwind, celltype, lam_alpha, lam_press)
    off_chip, in_chip = strips(*args)
    off_chip = swap(off_chip, XS, 1)
    in_chip = swap(in_chip, XS, 0)
    raw = shift(early(*args), LEN, 1)
    halo, down, upper = slabs(*args, off_chip, in_chip)
    above = shift(down, LEN, -1)
    below = shift(upper, LEN, 1)
    inside = inner(args, halo)
    grad_alpha, press, sums = relax(celltype, lam_alpha, owner, raw, below, above, inside)
    grad_velocity = faces(*args, halo, above)
    sums = total_over(sums, FIRST)
    sums = total_over(jnp.broadcast_to(sums[None], (size_of(SECOND), 128)), SECOND)
    cells = math.prod(alpha.shape) * size_of(LEN + XS)
    return (grad_alpha, grad_velocity, press, sums[:PORTS] / math.sqrt(cells))


def solution(mesh):
    parts = Mesh(mesh.devices.reshape(tuple(SIZES.values())), tuple(SIZES))
    field = P(LEN, XS, None)
    faces_spec = P(None, LEN, XS, None)
    in_specs = (field, faces_spec, faces_spec, field, P(XS, None), field, field)
    out_specs = (field, faces_spec, field, P())
    return jax.shard_map(body, mesh=parts, in_specs=in_specs, out_specs=out_specs, check_vma=False)
```
